256 devices in a mesh: section: 16 (over x, y), seq: 16 (over z, core).
Axes of the slice: x: 4, y: 4, z: 8, core: 2. Of those that a mesh axis runs over, the one named last changes fastest.
Arguments:
- inputs: bfloat16 [4, 8192, 1536], P(None, 'seq'), may hold values from -40 to 40
- weights: bfloat16 [2, 5, 1536, 1536], P(None, None, None, 'section'), may hold values from -0.0625 to 0.0625
- gains: float32 [2, 1536], replicated, may hold values from 0.1 to 1.9
Outputs:
- activations: bfloat16 [2, 4, 8192, 1536], P(None, None, 'seq', 'section')
The draws below stay inside these ranges and needn't reach their ends.
All inputs are finite; a program needn't handle non-finite values.
Results may differ from the reference program's by a relative error of at most 0.0044.
Values may be sent and summed in bfloat16 or wider, within the bound.
No kernel may reach another device: no remote copies, remote signals or barrier semaphores. Data moves between devices by JAX's collectives and lax.ppermute only.
A program may use at most 128 MiB of HBM per device.

```python
import math
import jax
import jax.numpy as jnp
from jax import lax

C = 1536
KW = 5
LAYERS = 2
MICRO = 4
LEN = 8192


def draw_inputs(key, part):
    first, second, third = jax.random.split(jax.random.fold_in(key, 11), 3)
    chan = jnp.exp(jax.random.uniform(second, (1, 1, C), jnp.float32, math.log(0.3), math.log(3.0)))
    place = jnp.exp(jax.random.uniform(third, (MICRO, LEN, 1), jnp.float32, math.log(0.3), math.log(3.0)))
    base = jnp.clip(jax.random.normal(first, (MICRO, LEN, C), jnp.float32), -4.0, 4.0)
    return (base * chan * place).astype(jnp.bfloat16)


def levels(own_key, shape, shards, least, top_value):
    level = 1.0
    for axis_at, shards_of in shards:
        heights = jax.random.uniform(jax.random.fold_in(jax.random.fold_in(own_key, 6), axis_at), (shards_of,), jnp.float32, least / len(shards), top_value / len(shards))
        level = level * jnp.repeat(jnp.exp(heights), shape[axis_at] // shards_of).reshape((-1,) + (1,) * (len(shape) - 1 - axis_at))
    return level


def centred(own_key, shape, scale, reach, cuts=(), held_as=jnp.bfloat16):
    drawn = jax.random.normal(own_key, shape, jnp.float32) * scale
    if len(cuts) > 0:
        drawn = levels(own_key, shape, cuts, -0.22, 0.18) * drawn
    return jnp.clip(drawn, min=-reach, max=reach).astype(held_as)


def setup_inputs(seed: int = 0) -> dict:
    key_list = jax.random.split(jax.random.key(seed), 4)
    inputs = draw_inputs(jax.random.fold_in(key_list[3], 71), 0)
    weights = centred(key_list[1], (LAYERS, KW, C, C), (KW * C) ** -0.5, 0.0625, ((3, 16),))
    gains = jnp.clip(1.0 + 0.18 * jax.random.normal(key_list[2], (LAYERS, C), jnp.float32), 0.1, 1.9)
    return dict(inputs=inputs, weights=weights, gains=gains)


def block(current, kernel, gain):
    values = current.astype(jnp.float32)
    scale = lax.rsqrt(lax.optimization_barrier(jnp.mean(values * values, axis=-1, keepdims=True)) + 1e-06)
    hidden = jax.nn.gelu(values * scale * gain).astype(jnp.bfloat16)
    padded = jnp.pad(hidden, ((0, 0), (2, 2), (0, 0)))
    total = jnp.zeros((MICRO * LEN, C), jnp.float32)
    for k in range(KW):
        window = padded[:, k:k + LEN, :].reshape(MICRO * LEN, C)
        total = total + jnp.dot(window, kernel[k], preferred_element_type=jnp.float32)
    return (values + total.reshape(MICRO, LEN, C)).astype(jnp.bfloat16)

def reference(inputs, weights, gains):

    def layer(current, pair):
        kernel, gain = pair
        nxt = block(current, kernel, gain)
        return (nxt, nxt)
    final, stacked = lax.scan(layer, inputs, (weights, gains))
    return stacked
```

```python
import functools
import jax
import jax.numpy as jnp
from jax import lax
from jax.experimental import pallas as pl
from jax.experimental.pallas import tpu as pltpu
from jax.sharding import Mesh, PartitionSpec as P

C = 1536
T = 96
R = 480
S = 512
B = 208
NT = (((1,), (1,)), ((), ()))


def gelu(z):
    return 0.5 * z * (1.0 + jnp.tanh(0.7978845608028654 * (z + 0.044715 * z * z * z)))


def combine(wide):
    n = wide.shape[1]
    total = wide[2 * T : 3 * T]
    for k in (0, 1, 3, 4):
        total = total + pltpu.roll(wide[k * T : (k + 1) * T], (2 - k) % n, 1)
    return total


def first_kernel(info, x_ref, halo_ref, gain_ref, w_ref, o_ref, h_ref, y_ref, hy_ref, hr_ref, base):
    i = pl.program_id(0)
    start = pl.multiple_of(info[0] * 128, 128)
    off = info[1]
    row = lax.broadcasted_iota(jnp.int32, (T, 256), 0)
    col = lax.broadcasted_iota(jnp.int32, (T, 256), 1)
    pick = jnp.where(col == row + off, 1.0, 0.0).astype(jnp.bfloat16)

    def hidden(v):
        v = v.astype(jnp.float32)
        scale = lax.rsqrt(jnp.sum(v * v, axis=-1, keepdims=True) * (1.0 / C) + 1e-06)
        return gelu(v * scale * gain_ref[...]).astype(jnp.bfloat16)

    @pl.when(i == 0)
    def _():
        hh = hidden(halo_ref[...])
        hy_ref[...] = jnp.zeros_like(hy_ref)
        hr_ref[...] = jnp.zeros_like(hr_ref)
        hy = lax.dot_general(w_ref[...], hh, NT, preferred_element_type=jnp.float32)
        hx = lax.dot_general(pick, halo_ref[:, pl.ds(start, 256)], NT, preferred_element_type=jnp.float32)
        hy_ref[:, 0:32] = hy
        hy_ref[2 * T : 3 * T, 0:32] += hx

    def body(r, _):
        at = pl.ds(pl.multiple_of(r * 16, 16), 16)
        h_ref[at, :] = hidden(x_ref[0, at, :])
        return _

    lax.fori_loop(0, S // 16, body, 0, unroll=2)
    y_ref[:, 128 : 128 + S] = lax.dot_general(w_ref[...], h_ref[...], NT, preferred_element_type=jnp.float32)
    y_ref[2 * T : 3 * T, 128 : 128 + S] += lax.dot_general(
        pick, x_ref[0, :, pl.ds(start, 256)], NT, preferred_element_type=jnp.float32
    )
    b = base + i
    y_ref[:, 0:128] = pltpu.roll(hy_ref[...], lax.rem(124 - 8 * b + 128, 128), 1)
    y_ref[:, 128 + S :] = pltpu.roll(hy_ref[...], lax.rem(256 - 8 * b - 4, 128), 1)
    out = combine(y_ref[...])
    o_ref[pl.ds(pl.multiple_of(i * T, 16), T), :] = out[:, 128 : 128 + S].astype(jnp.bfloat16)
    pad = jnp.zeros((32, 128), jnp.float32)
    left = jnp.concatenate([out[:, 0:128], pad], 0).T
    right = jnp.concatenate([out[:, 128 + S :], pad], 0).T
    keep_left = (info[2] > 0).astype(jnp.float32)
    keep_right = (info[3] > 0).astype(jnp.float32)
    line = jnp.concatenate(
        [left[126:127] * keep_left, left[127:128] * keep_left, right[0:1] * keep_right, right[1:2] * keep_right], 1
    )
    hr_ref[pl.ds(i, 1), :] = line
    o_ref[2 * T :, :] = hr_ref[...].astype(jnp.bfloat16)


def first(x, halo, gain, w, info, base):
    return pl.pallas_call(
        functools.partial(first_kernel, base=base),
        grid_spec=pltpu.PrefetchScalarGridSpec(
            num_scalar_prefetch=1,
            grid=(2,),
            in_specs=[
                pl.BlockSpec((1, S, C), lambda i, info: (base + i, 0, 0)),
                pl.BlockSpec((32, C), lambda i, info: (0, 0)),
                pl.BlockSpec((1, C), lambda i, info: (0, 0)),
                pl.BlockSpec((R, C), lambda i, info: (0, 0)),
            ],
            out_specs=pl.BlockSpec((B, S), lambda i, info: (0, 0)),
            scratch_shapes=[
                pltpu.VMEM((S, C), jnp.bfloat16),
                pltpu.VMEM((R, S + 256), jnp.float32),
                pltpu.VMEM((R, 128), jnp.float32),
                pltpu.VMEM((16, S), jnp.float32),
            ],
        ),
        out_shape=jax.ShapeDtypeStruct((B, S), jnp.bfloat16),
        compiler_params=pltpu.CompilerParams(dimension_semantics=("arbitrary",), vmem_limit_bytes=40 << 20),
        cost_estimate=pl.CostEstimate(flops=4 * S * R * C, bytes_accessed=2 * S * C * 2 + R * C * 2, transcendentals=2 * S * C),
        name="first",
    )(info, x, halo, gain, w)


def second_kernel(order, a0, a1, a2, a3, a4, gain_ref, w_ref, o_ref, h_ref, y_ref, e_ref, sq_ref):
    refs = [(a0, 4, 0), (a1, 4, 4), (a2, 4, 8), (a3, 2, 12), (a4, 2, 14)]
    n = 2 * S + 128
    sq_ref[...] = jnp.zeros_like(sq_ref)

    for ref, count, at in refs:
        def gather(k, _, ref=ref, at=at):
            row = pl.multiple_of(k * B, 16)
            lines = ref[pl.ds(row + 2 * T, 16), :].astype(jnp.float32)
            tile = jnp.concatenate(
                [lines[j : j + 1, 128 * q : 128 * q + 128] for j in range(2) for q in range(4)]
                + [jnp.zeros((120, 128), jnp.float32)],
                0,
            )
            edge = tile.T[0:T]
            e_ref[pl.ds(pl.multiple_of((at + k) * T, 16), T), :] = edge
            sq = edge * edge
            acc = sq_ref[:, 2 * S :]
            for g in range(T // 8):
                acc = acc + sq[8 * g : 8 * g + 8]
            sq_ref[:, 2 * S :] = acc
            for j in range(2):
                v = ref[pl.ds(row + j * T, T), :].astype(jnp.float32)
                v = v * v
                acc = sq_ref[:, j * S : j * S + S]
                for g in range(T // 8):
                    acc = acc + v[8 * g : 8 * g + 8]
                sq_ref[:, j * S : j * S + S] = acc
            return _

        lax.fori_loop(0, count, gather, 0)

    total = jnp.sum(sq_ref[...], axis=0, keepdims=True)
    scale = lax.rsqrt(total * (1.0 / C) + 1e-06)
    sq_ref[...] = jnp.broadcast_to(scale, (8, n))

    for ref, count, at in refs:
        def apply(k, _, ref=ref, at=at):
            row = pl.multiple_of(k * B, 16)
            dest = pl.multiple_of(order[at + k] * T, 16)
            gain = gain_ref[pl.ds(dest, T), :]
            for j in range(2):
                for q in range(4):
                    lane = slice(j * S + 128 * q, j * S + 128 * q + 128)
                    v = ref[pl.ds(row + j * T, T), 128 * q : 128 * q + 128].astype(jnp.float32)
                    h_ref[pl.ds(dest, T), lane] = gelu(v * sq_ref[0:1, lane] * gain).astype(jnp.bfloat16)
            v = e_ref[pl.ds(pl.multiple_of((at + k) * T, 16), T), :]
            h_ref[pl.ds(dest, T), 2 * S :] = gelu(v * sq_ref[0:1, 2 * S :] * gain).astype(jnp.bfloat16)
            return _

        lax.fori_loop(0, count, apply, 0)

    y_ref[...] = jnp.dot(w_ref[...], h_ref[...], preferred_element_type=jnp.float32)
    for j in range(2):
        edge = y_ref[:, 2 * S :]
        wide = jnp.concatenate(
            [pltpu.roll(edge, 126 - 4 * j, 1), y_ref[:, j * S : j * S + S], pltpu.roll(edge, 126 - 4 * j, 1)], 1
        )
        out = combine(wide)[:, 128 : 128 + S] + a0[j * T : j * T + T, :].astype(jnp.float32)
        o_ref[j * T : j * T + T, :] = out.astype(jnp.bfloat16)


def second(parts, gain, w, order):
    vmem = pl.BlockSpec(memory_space=pltpu.VMEM)
    n = 2 * S + 128
    return pl.pallas_call(
        second_kernel,
        in_specs=[pl.BlockSpec(memory_space=pltpu.SMEM)] + [vmem] * 7,
        out_specs=vmem,
        out_shape=jax.ShapeDtypeStruct((2 * T, S), jnp.bfloat16),
        scratch_shapes=[
            pltpu.VMEM((C, n), jnp.bfloat16),
            pltpu.VMEM((R, n), jnp.float32),
            pltpu.VMEM((C, 128), jnp.float32),
            pltpu.VMEM((8, n), jnp.float32),
        ],
        compiler_params=pltpu.CompilerParams(vmem_limit_bytes=40 << 20),
        cost_estimate=pl.CostEstimate(flops=4 * S * R * C, bytes_accessed=2 * S * C * 2 + R * C * 2, transcendentals=2 * S * C),
        name="second",
    )(order, *parts, gain, w)


def shift(value, axis, d):
    return lax.ppermute(value, axis, [(i, (i + d) % 4) for i in range(4)])


def gather(block, f, s):
    below, above = shift(block, f, 1), shift(block, f, -1)
    far0, far1 = shift(below[:T], f, 1), shift(above[T:], f, -1)
    column = jnp.concatenate([block, below, above, far0, far1], 0)
    left, right = shift(column, s, 1), shift(column, s, -1)
    return [column, left, right, shift(left[: 2 * B], s, 1), shift(right[2 * B :], s, -1)]


def piece_order(f, s):
    def index(df, ds):
        at = {f: (lax.axis_index(f) + df) % 4, s: (lax.axis_index(s) + ds) % 4}
        return at["x"] * 4 + at["y"]

    rel = (0, -1, 1, 2)
    items = [index(r, d) for d in (0, -1, 1) for r in rel] + [index(r, 2) for r in rel]
    return jnp.stack(items).astype(jnp.int32)


def local(inputs, weights, gains):
    x, y = lax.axis_index("x"), lax.axis_index("y")
    sec = x * 4 + y
    seq = lax.axis_index("z") * 2 + lax.axis_index("core")
    w = weights.transpose(0, 1, 3, 2).reshape(2, R, C)
    up = [(i, i + 1) for i in range(15)]
    down = [(i + 1, i) for i in range(15)]
    before = lax.ppermute(inputs[:, S - 4 :], ("z", "core"), up)
    after = lax.ppermute(inputs[:, :4], ("z", "core"), down)
    halo = jnp.concatenate([before, after], 1).reshape(32, C)
    block = jnp.minimum(sec * T // 128, 10)
    info = jnp.stack([block, sec * T - block * 128, seq, 15 - seq]).astype(jnp.int32)
    g0 = gains[0:1]
    g1 = jnp.broadcast_to(gains[1][:, None], (C, 128))
    half0 = first(inputs, halo, g0, w[0], info, 0)
    half1 = first(inputs, halo, g0, w[0], info, 2)
    got0 = gather(half0, "y", "x")
    got1 = gather(half1, "x", "y")
    out0 = second(got0, g1, w[1], piece_order("y", "x"))
    out1 = second(got1, g1, w[1], piece_order("x", "y"))
    out = jnp.concatenate([half0[: 2 * T], half1[: 2 * T], out0, out1], 0)
    return out.reshape(2, 4, T, S).transpose(0, 1, 3, 2)


def solution(mesh):
    grid = Mesh(mesh.devices.reshape(4, 4, 8, 2), ("x", "y", "z", "core"))
    in_specs = (P(None, ("z", "core"), None), P(None, None, None, ("x", "y")), P())
    out_specs = P(None, None, ("z", "core"), ("x", "y"))
    return jax.shard_map(local, mesh=grid, in_specs=in_specs, out_specs=out_specs, check_vma=False)
```

```python
import functools
import jax
import jax.numpy as jnp
from jax import lax
from jax.experimental import pallas as pl
from jax.experimental.pallas import tpu as pltpu
from jax.sharding import Mesh, PartitionSpec as P

C = 1536
T = 96
R = 480
S = 512
B = 208
Q = 384
N = 1152
NT = (((1,), (1,)), ((), ()))


def gelu(z):
    return 0.5 * z * (1.0 + jnp.tanh(0.7978845608028654 * (z + 0.044715 * z * z * z)))


def combine(wide):
    n = wide.shape[1]
    total = wide[2 * T : 3 * T]
    for k in (0, 1, 3, 4):
        total = total + pltpu.roll(wide[k * T : (k + 1) * T], (2 - k) % n, 1)
    return total


def first_kernel(info, x_ref, halo_ref, gain_ref, w_ref, o_ref, sq_ref, h_ref, y_ref, hy_ref, hr_ref, base):
    i = pl.program_id(0)
    start = pl.multiple_of(info[0] * 128, 128)
    off = info[1]
    row = lax.broadcasted_iota(jnp.int32, (T, 256), 0)
    col = lax.broadcasted_iota(jnp.int32, (T, 256), 1)
    pick = jnp.where(col == row + off, 1.0, 0.0).astype(jnp.bfloat16)

    def hidden(v):
        v = v.astype(jnp.float32)
        scale = lax.rsqrt(jnp.sum(v * v, axis=-1, keepdims=True) * (1.0 / C) + 1e-06)
        return gelu(v * scale * gain_ref[...]).astype(jnp.bfloat16)

    @pl.when(i == 0)
    def _():
        hh = hidden(halo_ref[...])
        hy_ref[...] = jnp.zeros_like(hy_ref)
        hr_ref[...] = jnp.zeros_like(hr_ref)
        sq_ref[...] = jnp.zeros_like(sq_ref)
        hy = lax.dot_general(w_ref[...], hh, NT, preferred_element_type=jnp.float32)
        hx = lax.dot_general(pick, halo_ref[:, pl.ds(start, 256)], NT, preferred_element_type=jnp.float32)
        hy_ref[:, 0:32] = hy
        hy_ref[2 * T : 3 * T, 0:32] += hx

    def body(r, _):
        at = pl.ds(pl.multiple_of(r * 16, 16), 16)
        h_ref[at, :] = hidden(x_ref[0, at, :])
        return _

    lax.fori_loop(0, S // 16, body, 0, unroll=2)
    y_ref[:, 128 : 128 + S] = lax.dot_general(w_ref[...], h_ref[...], NT, preferred_element_type=jnp.float32)
    y_ref[2 * T : 3 * T, 128 : 128 + S] += lax.dot_general(
        pick, x_ref[0, :, pl.ds(start, 256)], NT, preferred_element_type=jnp.float32
    )
    b = base + i
    y_ref[:, 0:128] = pltpu.roll(hy_ref[...], lax.rem(124 - 8 * b + 128, 128), 1)
    y_ref[:, 128 + S :] = pltpu.roll(hy_ref[...], lax.rem(256 - 8 * b - 4, 128), 1)
    out = combine(y_ref[...])
    out = out.astype(jnp.bfloat16)
    o_ref[pl.ds(pl.multiple_of(i * T, 16), T), :] = out[:, 128 : 128 + S]
    out = out.astype(jnp.float32)
    squares = jnp.sum(out * out, axis=0, keepdims=True)
    sq_ref[:, pl.ds(pl.multiple_of(i * S, 128), S)] = squares[:, 128 : 128 + S]
    pad = jnp.zeros((32, 128), jnp.float32)
    left = jnp.concatenate([out[:, 0:128], pad], 0).T
    right = jnp.concatenate([out[:, 128 + S :], pad], 0).T
    keep_left = (info[2] > 0).astype(jnp.float32)
    keep_right = (info[3] > 0).astype(jnp.float32)
    lane = lax.broadcasted_iota(jnp.int32, (1, 128), 1) - 4 * i
    turn = lax.rem(4 * i + 2, 128)
    edge = jnp.where((lane == 0) | (lane == 1), pltpu.roll(squares[:, 0:128], turn, 1) * keep_left, 0.0)
    edge += jnp.where((lane == 2) | (lane == 3), pltpu.roll(squares[:, 128 + S :], turn, 1) * keep_right, 0.0)
    sq_ref[:, 2 * S :] += edge
    line = jnp.concatenate(
        [left[126:127] * keep_left, left[127:128] * keep_left, right[0:1] * keep_right, right[1:2] * keep_right], 1
    )
    hr_ref[pl.ds(i, 1), :] = line
    o_ref[2 * T :, :] = hr_ref[...].astype(jnp.bfloat16)


def first(x, halo, gain, w, info, base):
    return pl.pallas_call(
        functools.partial(first_kernel, base=base),
        grid_spec=pltpu.PrefetchScalarGridSpec(
            num_scalar_prefetch=1,
            grid=(2,),
            in_specs=[
                pl.BlockSpec((1, S, C), lambda i, info: (base + i, 0, 0)),
                pl.BlockSpec((32, C), lambda i, info: (0, 0)),
                pl.BlockSpec((1, C), lambda i, info: (0, 0)),
                pl.BlockSpec((R, C), lambda i, info: (0, 0)),
            ],
            out_specs=[pl.BlockSpec((B, S), lambda i, info: (0, 0)), pl.BlockSpec((1, N), lambda i, info: (0, 0))],
            scratch_shapes=[
                pltpu.VMEM((S, C), jnp.bfloat16),
                pltpu.VMEM((R, S + 256), jnp.float32),
                pltpu.VMEM((R, 128), jnp.float32),
                pltpu.VMEM((16, S), jnp.float32),
            ],
        ),
        out_shape=[jax.ShapeDtypeStruct((B, S), jnp.bfloat16), jax.ShapeDtypeStruct((1, N), jnp.float32)],
        compiler_params=pltpu.CompilerParams(dimension_semantics=("arbitrary",), vmem_limit_bytes=40 << 20),
        cost_estimate=pl.CostEstimate(flops=4 * S * R * C, bytes_accessed=2 * S * C * 2 + R * C * 2, transcendentals=2 * S * C),
        name="first",
    )(info, x, halo, gain, w)


def prep_kernel(pos, w_ref, *refs):
    outs, perm = refs[:8], refs[8]
    for r in range(0, R, 96):
        v = w_ref[r : r + 96, :].astype(jnp.float32)
        cols = [v[:, (a * 4 + b) * T : (a * 4 + b) * T + T] for b in range(4) for a in range(4)]
        perm[r : r + 96, :] = jnp.concatenate(cols, 1).astype(jnp.bfloat16)
    for n, (src, at) in enumerate(((perm, pos[1]), (w_ref, pos[0]))):
        for m, d in enumerate((0, 1, 3, 2)):
            lane = pl.multiple_of(lax.rem(at + d, 4) * Q, 128)
            outs[n * 4 + m][...] = src[:, pl.ds(lane, Q)]


def prep(w, pos):
    vmem = pl.BlockSpec(memory_space=pltpu.VMEM)
    return pl.pallas_call(
        prep_kernel,
        in_specs=[pl.BlockSpec(memory_space=pltpu.SMEM), vmem],
        out_specs=[vmem] * 8,
        out_shape=[jax.ShapeDtypeStruct((R, Q), jnp.bfloat16)] * 8,
        scratch_shapes=[pltpu.VMEM((R, C), jnp.bfloat16)],
        compiler_params=pltpu.CompilerParams(vmem_limit_bytes=24 << 20),
        cost_estimate=pl.CostEstimate(flops=0, bytes_accessed=6 * R * C, transcendentals=0),
        name="prep",
    )(pos, w)


def partial_sum(w_ref, h_ref, y_ref):
    y_ref[...] = jnp.dot(w_ref[...], h_ref[...], preferred_element_type=jnp.float32)
    outs = []
    for j in range(2):
        edge = pltpu.roll(y_ref[:, 2 * S :], 126 - 4 * j, 1)
        wide = jnp.concatenate([edge, y_ref[:, j * S : j * S + S], edge], 1)
        outs.append(combine(wide)[:, 128 : 128 + S])
    return outs


def far_kernel(order, a0, a1, a2, a3, a4, sq_ref, gain_ref, w_ref, h_ref, far0_ref, far1_ref, y_ref, s_ref):
    s_ref[...] = jnp.broadcast_to(lax.rsqrt(sq_ref[...] * (1.0 / C) + 1e-06), s_ref.shape)

    def put(piece, halves, lines):
        dest = pl.multiple_of(order[piece] * T, 16)
        gain = gain_ref[pl.ds(dest, T), :]
        lines = lines.astype(jnp.float32)
        tile = jnp.concatenate(
            [lines[j : j + 1, 128 * q : 128 * q + 128] for j in range(2) for q in range(4)]
            + [jnp.zeros((120, 128), jnp.float32)],
            0,
        )
        h_ref[pl.ds(dest, T), 2 * S :] = gelu(tile.T[0:T] * s_ref[0:1, 2 * S :] * gain).astype(jnp.bfloat16)
        for j in range(2):
            for q in range(4):
                lane = slice(j * S + 128 * q, j * S + 128 * q + 128)
                v = halves[j][:, 128 * q : 128 * q + 128].astype(jnp.float32)
                h_ref[pl.ds(dest, T), lane] = gelu(v * s_ref[0:1, lane] * gain).astype(jnp.bfloat16)

    for piece, ref in enumerate((a0, a1, a2)):
        put(piece, (ref[0:T, :], ref[T : 2 * T, :]), ref[2 * T :, :])
    put(3, (a3[...], a4[0:T, :]), a4[T:, :])
    far0, far1 = partial_sum(w_ref, h_ref, y_ref)
    far0_ref[...] = far0.astype(jnp.bfloat16)
    far1_ref[...] = far1.astype(jnp.bfloat16)


def far_stage(order, parts, sq, gain, w):
    vmem = pl.BlockSpec(memory_space=pltpu.VMEM)
    return pl.pallas_call(
        far_kernel,
        in_specs=[pl.BlockSpec(memory_space=pltpu.SMEM)] + [vmem] * 8,
        out_specs=[vmem] * 3,
        out_shape=[
            jax.ShapeDtypeStruct((Q, N), jnp.bfloat16),
            jax.ShapeDtypeStruct((T, S), jnp.bfloat16),
            jax.ShapeDtypeStruct((T, S), jnp.bfloat16),
        ],
        scratch_shapes=[pltpu.VMEM((R, N), jnp.float32), pltpu.VMEM((8, N), jnp.float32)],
        compiler_params=pltpu.CompilerParams(vmem_limit_bytes=24 << 20),
        cost_estimate=pl.CostEstimate(flops=2 * R * Q * N, bytes_accessed=4 * Q * N, transcendentals=Q * N),
        name="far",
    )(order, *parts, sq, gain, w)


def near_kernel(h_ref, wp_ref, wm_ref, r0_ref, r1_ref, p_ref, m_ref, y_ref):
    out = partial_sum(wp_ref, h_ref, y_ref)
    p_ref[0:T, :] = (out[0] + r0_ref[...].astype(jnp.float32)).astype(jnp.bfloat16)
    p_ref[T:, :] = out[1].astype(jnp.bfloat16)
    out = partial_sum(wm_ref, h_ref, y_ref)
    m_ref[0:T, :] = out[0].astype(jnp.bfloat16)
    m_ref[T:, :] = (out[1] + r1_ref[...].astype(jnp.float32)).astype(jnp.bfloat16)


def near_stage(h, wp, wm, r0, r1):
    vmem = pl.BlockSpec(memory_space=pltpu.VMEM)
    return pl.pallas_call(
        near_kernel,
        in_specs=[vmem] * 5,
        out_specs=[vmem] * 2,
        out_shape=[jax.ShapeDtypeStruct((2 * T, S), jnp.bfloat16)] * 2,
        scratch_shapes=[pltpu.VMEM((R, N), jnp.float32)],
        compiler_params=pltpu.CompilerParams(vmem_limit_bytes=24 << 20),
        cost_estimate=pl.CostEstimate(flops=4 * R * Q * N, bytes_accessed=4 * Q * N, transcendentals=0),
        name="near",
    )(h, wp, wm, r0, r1)


def own_kernel(h_ref, w_ref, a_ref, o_ref, y_ref):
    out = partial_sum(w_ref, h_ref, y_ref)
    for j in range(2):
        o_ref[j * T : j * T + T, :] = out[j] + a_ref[j * T : j * T + T, :].astype(jnp.float32)


def own_stage(h, w, a):
    vmem = pl.BlockSpec(memory_space=pltpu.VMEM)
    return pl.pallas_call(
        own_kernel,
        in_specs=[vmem] * 3,
        out_specs=vmem,
        out_shape=jax.ShapeDtypeStruct((2 * T, S), jnp.float32),
        scratch_shapes=[pltpu.VMEM((R, N), jnp.float32)],
        compiler_params=pltpu.CompilerParams(vmem_limit_bytes=24 << 20),
        cost_estimate=pl.CostEstimate(flops=2 * R * Q * N, bytes_accessed=4 * Q * N, transcendentals=0),
        name="own",
    )(h, w, a)


def shift(value, axis, d):
    return lax.ppermute(value, axis, [(i, (i + d) % 4) for i in range(4)])


def gather(block, f):
    below, above = shift(block, f, 1), shift(block, f, -1)
    return [block, below, above, shift(below[:T], f, 1), shift(above[T:], f, -1)]


def spread(weights, g):
    return shift(weights[2], g, -1), shift(weights[1], g, 1), shift(weights[3], g, 2)


def local(inputs, weights, gains):
    x, y = lax.axis_index("x"), lax.axis_index("y")
    sec = x * 4 + y
    seq = lax.axis_index("z") * 2 + lax.axis_index("core")
    w = weights.transpose(0, 1, 3, 2).reshape(2, R, C)
    up = [(i, i + 1) for i in range(15)]
    down = [(i + 1, i) for i in range(15)]
    before = lax.ppermute(inputs[:, S - 4 :], ("z", "core"), up)
    after = lax.ppermute(inputs[:, :4], ("z", "core"), down)
    halo = jnp.concatenate([before, after], 1).reshape(32, C)
    send = prep(w[1], jnp.stack([x, y]).astype(jnp.int32))
    w_y = (send[0],) + spread(send[:4], "y")
    w_x = (send[4],) + spread(send[4:], "x")
    block = jnp.minimum(sec * T // 128, 10)
    info = jnp.stack([block, sec * T - block * 128, seq, 15 - seq]).astype(jnp.int32)
    g0 = gains[0:1]
    g1 = gains[1].reshape(4, 4, T)
    g_x = jnp.broadcast_to(lax.dynamic_index_in_dim(g1, y, 1, False).reshape(Q, 1), (Q, 128))
    g_y = jnp.broadcast_to(lax.dynamic_index_in_dim(g1, x, 0, False).reshape(Q, 1), (Q, 128))
    half0, sq0 = first(inputs, halo, g0, w[0], info, 0)
    half1, sq1 = first(inputs, halo, g0, w[0], info, 2)
    got0 = gather(half0, "x")
    got1 = gather(half1, "y")
    sq = jnp.concatenate([sq0, sq1], 0)
    for axis in ("x", "y"):
        sq = sq + lax.ppermute(sq, axis, [(i, i ^ 1) for i in range(4)])
        sq = sq + lax.ppermute(sq, axis, [(i, i ^ 2) for i in range(4)])
    outs = []
    for got, own, at, weight, gain, line, g in (
        (got0, half0, x, w_y, g_x, sq[0:1], "y"),
        (got1, half1, y, w_x, g_y, sq[1:2], "x"),
    ):
        order = jnp.stack([at, (at + 3) % 4, (at + 1) % 4, (at + 2) % 4]).astype(jnp.int32)
        h, far0, far1 = far_stage(order, got, line, gain, weight[3])
        plus, minus = near_stage(h, weight[1], weight[2], shift(far0, g, 1), shift(far1, g, -1))
        base = own_stage(h, weight[0], own[: 2 * T])
        total = base + shift(plus, g, 1).astype(jnp.float32) + shift(minus, g, -1).astype(jnp.float32)
        outs.append(total.astype(jnp.bfloat16))
    out = jnp.concatenate([half0[: 2 * T], half1[: 2 * T]] + outs, 0)
    return out.reshape(2, 4, T, S).transpose(0, 1, 3, 2)


def solution(mesh):
    grid = Mesh(mesh.devices.reshape(4, 4, 8, 2), ("x", "y", "z", "core"))
    in_specs = (P(None, ("z", "core"), None), P(None, None, None, ("x", "y")), P())
    out_specs = P(None, None, ("z", "core"), ("x", "y"))
    return jax.shard_map(local, mesh=grid, in_specs=in_specs, out_specs=out_specs, check_vma=False)
```

```python
import functools
import jax
import jax.numpy as jnp
from jax import lax
from jax.experimental import pallas as pl
from jax.experimental.pallas import tpu as pltpu
from jax.sharding import Mesh, PartitionSpec as P

C = 1536
T = 96
R = 480
S = 512
M = 4
B = 400
HB = 192
Q = 384
HR = 240
N = M * S + 128
NT = (((1,), (1,)), ((), ()))


def whole(*shape):
    return pl.BlockSpec(shape, lambda i, *_: (0,) * len(shape))


def gelu(z):
    half = 0.5 * z
    return half + half * jnp.tanh(z * (0.7978845608028654 + 0.035677408136300125 * (z * z)))


def combine(wide):
    n = wide.shape[1]
    total = wide[2 * T : 3 * T]
    for k in (0, 1, 3, 4):
        total = total + pltpu.roll(wide[k * T : (k + 1) * T], (2 - k) % n, 1)
    return total


def first_kernel(info, x_ref, halo_ref, gain_ref, w_ref, o_ref, sq_ref, h_ref, y_ref, hy_ref, hr_ref):
    i = pl.program_id(0)
    start = pl.multiple_of(info[0] * 128, 128)
    off = info[1]
    row = lax.broadcasted_iota(jnp.int32, (T, 256), 0)
    col = lax.broadcasted_iota(jnp.int32, (T, 256), 1)
    pick = jnp.where(col == row + off, 1.0, 0.0).astype(jnp.bfloat16)

    def hidden(v):
        v = v.astype(jnp.float32)
        scale = lax.rsqrt(jnp.sum(v * v, axis=-1, keepdims=True) * (1.0 / C) + 1e-06)
        return gelu(v * scale * gain_ref[...]).astype(jnp.bfloat16)

    @pl.when(i == 0)
    def _():
        hh = hidden(halo_ref[...])
        hy_ref[...] = jnp.zeros_like(hy_ref)
        hr_ref[...] = jnp.zeros_like(hr_ref)
        sq_ref[...] = jnp.zeros_like(sq_ref)
        hy = lax.dot_general(w_ref[...], hh, NT, preferred_element_type=jnp.float32)
        hx = lax.dot_general(pick, halo_ref[:, pl.ds(start, 256)], NT, preferred_element_type=jnp.float32)
        hy_ref[:, 0:32] = hy
        hy_ref[2 * T : 3 * T, 0:32] += hx

    window = pl.ds(start, 256)
    for c in range(2):
        for r in range(c * 256, c * 256 + 256, 16):
            h_ref[r : r + 16, :] = hidden(x_ref[0, r : r + 16, :])
        at = slice(c * 256, c * 256 + 256)
        to = slice(128 + c * 256, 384 + c * 256)
        y_ref[:, to] = lax.dot_general(w_ref[...], h_ref[at, :], NT, preferred_element_type=jnp.float32)
        y_ref[2 * T : 3 * T, to] += lax.dot_general(
            pick, x_ref[0, at, window], NT, preferred_element_type=jnp.float32
        )
    y_ref[:, 0:128] = pltpu.roll(hy_ref[...], lax.rem(252 - 8 * i, 128), 1)
    y_ref[:, 128 + S :] = pltpu.roll(hy_ref[...], lax.rem(252 - 8 * i, 128), 1)
    out = combine(y_ref[...])
    out = out.astype(jnp.bfloat16)
    o_ref[pl.ds(pl.multiple_of(i * T, 16), T), :] = out[:, 128 : 128 + S]
    out = out.astype(jnp.float32)
    squares = jnp.sum(out * out, axis=0, keepdims=True)
    sq_ref[:, pl.ds(pl.multiple_of(i * S, 128), S)] = squares[:, 128 : 128 + S]
    pad = jnp.zeros((32, 128), jnp.float32)
    left = jnp.concatenate([out[:, 0:128], pad], 0).T
    right = jnp.concatenate([out[:, 128 + S :], pad], 0).T
    keep_left = (info[2] > 0).astype(jnp.float32)
    keep_right = (info[3] > 0).astype(jnp.float32)
    lane = lax.broadcasted_iota(jnp.int32, (1, 128), 1) - 4 * i
    turn = lax.rem(4 * i + 2, 128)
    edge = jnp.where((lane == 0) | (lane == 1), pltpu.roll(squares[:, 0:128], turn, 1) * keep_left, 0.0)
    edge += jnp.where((lane == 2) | (lane == 3), pltpu.roll(squares[:, 128 + S :], turn, 1) * keep_right, 0.0)
    sq_ref[:, M * S :] += edge
    line = jnp.concatenate(
        [left[126:127] * keep_left, left[127:128] * keep_left, right[0:1] * keep_right, right[1:2] * keep_right], 1
    )
    hr_ref[pl.ds(i, 1), :] = line
    o_ref[M * T :, :] = hr_ref[...].astype(jnp.bfloat16)


def first(x, halo, gain, w, info):
    return pl.pallas_call(
        first_kernel,
        grid_spec=pltpu.PrefetchScalarGridSpec(
            num_scalar_prefetch=1,
            grid=(M,),
            in_specs=[
                pl.BlockSpec((1, S, C), lambda i, info: (i, 0, 0)),
                whole(32, C),
                whole(1, C),
                pl.BlockSpec((None, R, C), lambda i, info: (0, 0, 0)),
            ],
            out_specs=[whole(B, S), whole(1, N)],
            scratch_shapes=[
                pltpu.VMEM((S, C), jnp.bfloat16),
                pltpu.VMEM((R, S + 256), jnp.float32),
                pltpu.VMEM((R, 128), jnp.float32),
                pltpu.VMEM((16, S), jnp.float32),
            ],
        ),
        out_shape=[jax.ShapeDtypeStruct((B, S), jnp.bfloat16), jax.ShapeDtypeStruct((1, N), jnp.float32)],
        compiler_params=pltpu.CompilerParams(dimension_semantics=("arbitrary",), vmem_limit_bytes=32 << 20),
        cost_estimate=pl.CostEstimate(flops=2 * M * S * R * C, bytes_accessed=2 * M * S * C, transcendentals=M * S * C),
        name="first",
    )(info, x, halo, gain, w)


def prep_kernel(core, w_ref, o_ref):
    for r in range(0, HR, 80):
        v = w_ref[r : r + 80, :].astype(jnp.float32)
        for b in range(4):
            cols = [v[:, (a * 4 + b) * T : (a * 4 + b) * T + T] for a in range(4)]
            o_ref[b, r : r + 80, :] = jnp.concatenate(cols, 1).astype(jnp.bfloat16)


def prep(core, w):
    return pl.pallas_call(
        prep_kernel,
        grid_spec=pltpu.PrefetchScalarGridSpec(
            num_scalar_prefetch=1,
            grid=(1,),
            in_specs=[pl.BlockSpec((None, HR, C), lambda i, core: (1, core[0], 0))],
            out_specs=whole(4, HR, Q),
        ),
        out_shape=jax.ShapeDtypeStruct((4, HR, Q), jnp.bfloat16),
        compiler_params=pltpu.CompilerParams(vmem_limit_bytes=16 << 20),
        cost_estimate=pl.CostEstimate(flops=0, bytes_accessed=4 * HR * C, transcendentals=0),
        name="prep",
    )(core, w)


def partial_sum(core, mine_ref, other_ref, h_ref, y_ref):
    at = pl.multiple_of(core * HR, 16)
    y_ref[pl.ds(at, HR), :] = jnp.dot(mine_ref[...], h_ref[...], preferred_element_type=jnp.float32)
    at = pl.multiple_of(HR - core * HR, 16)
    y_ref[pl.ds(at, HR), :] = jnp.dot(other_ref[...], h_ref[...], preferred_element_type=jnp.float32)
    outs = []
    for j in range(M):
        edge = pltpu.roll(y_ref[:, M * S :], 126 - 4 * j, 1)
        wide = jnp.concatenate([edge, y_ref[:, j * S : j * S + S], edge], 1)
        outs.append(combine(wide)[:, 128 : 128 + S])
    return outs


def far_kernel(order, a0, a1, a2, a3, a4, sq_ref, gain_ref, wa_ref, wb_ref, h_ref, far0_ref, far1_ref, y_ref, s_ref):
    s_ref[...] = jnp.broadcast_to(lax.rsqrt(sq_ref[...] * (1.0 / C) + 1e-06), s_ref.shape)

    def put(piece, parts, lines):
        dest = pl.multiple_of(order[piece] * T, 16)
        gain = gain_ref[pl.ds(dest, T), :]
        lines = lines.astype(jnp.float32)
        tile = jnp.concatenate(
            [lines[j : j + 1, 128 * q : 128 * q + 128] for j in range(M) for q in range(4)]
            + [jnp.zeros((112, 128), jnp.float32)],
            0,
        )
        h_ref[pl.ds(dest, T), M * S :] = gelu(tile.T[0:T] * s_ref[0:1, M * S :] * gain).astype(jnp.bfloat16)
        for j in range(M):
            ref, row = parts[j]
            for q in range(4):
                lane = slice(j * S + 128 * q, j * S + 128 * q + 128)
                v = ref[row : row + T, 128 * q : 128 * q + 128].astype(jnp.float32)
                h_ref[pl.ds(dest, T), lane] = gelu(v * s_ref[0:1, lane] * gain).astype(jnp.bfloat16)

    for piece, ref in enumerate((a0, a1, a2)):
        put(piece, [(ref, j * T) for j in range(M)], ref[M * T :, :])
    put(3, [(a3, 0), (a3, T), (a4, 0), (a4, T)], a4[HB:, :])
    out = partial_sum(order[8], wa_ref, wb_ref, h_ref, y_ref)
    for j in range(2):
        far0_ref[j * T : j * T + T, :] = out[j].astype(jnp.bfloat16)
        far1_ref[j * T : j * T + T, :] = out[j + 2].astype(jnp.bfloat16)


def picked(k):
    return [pl.BlockSpec((None, HR, Q), lambda i, order: (order[k], 0, 0))] * 2


def stage(kernel, order, args, in_specs, outs, scratch, flops, name):
    return pl.pallas_call(
        kernel,
        grid_spec=pltpu.PrefetchScalarGridSpec(
            num_scalar_prefetch=1,
            grid=(1,),
            in_specs=in_specs,
            out_specs=[whole(*o.shape) for o in outs],
            scratch_shapes=[pltpu.VMEM((R, N), jnp.float32)] + scratch,
        ),
        out_shape=outs,
        compiler_params=pltpu.CompilerParams(vmem_limit_bytes=32 << 20),
        cost_estimate=pl.CostEstimate(flops=flops, bytes_accessed=4 * Q * N, transcendentals=0),
        name=name,
    )(order, *args)


def near_kernel(order, h_ref, pa_ref, pb_ref, ma_ref, mb_ref, r0_ref, r1_ref, p_ref, m_ref, y_ref):
    out = partial_sum(order[8], pa_ref, pb_ref, h_ref, y_ref)
    for j in range(M):
        at = slice(j * T, j * T + T)
        value = out[j] + r0_ref[at, :].astype(jnp.float32) if j < 2 else out[j]
        p_ref[at, :] = value.astype(jnp.bfloat16)
    out = partial_sum(order[8], ma_ref, mb_ref, h_ref, y_ref)
    for j in range(M):
        at = slice(j * T, j * T + T)
        value = out[j] + r1_ref[j * T - HB : j * T - HB + T, :].astype(jnp.float32) if j >= 2 else out[j]
        m_ref[at, :] = value.astype(jnp.bfloat16)


def own_kernel(order, h_ref, wa_ref, wb_ref, a_ref, o_ref, y_ref):
    out = partial_sum(order[8], wa_ref, wb_ref, h_ref, y_ref)
    for j in range(M):
        at = slice(j * T, j * T + T)
        o_ref[at, :] = out[j] + a_ref[at, :].astype(jnp.float32)


def shift(value, axis, d):
    return lax.ppermute(value, axis, [(i, (i + d) % 4) for i in range(4)])


def local(inputs, weights, gains):
    x, y, core = lax.axis_index("x"), lax.axis_index("y"), lax.axis_index("core")
    sec = x * 4 + y
    seq = lax.axis_index("z") * 2 + core
    w = weights.transpose(0, 1, 3, 2).reshape(2, R, C)
    up = [(i, i + 1) for i in range(15)]
    down = [(i + 1, i) for i in range(15)]
    before = lax.ppermute(inputs[:, S - 4 :], ("z", "core"), up)
    after = lax.ppermute(inputs[:, :4], ("z", "core"), down)
    halo = jnp.concatenate([before, after], 1).reshape(32, C)
    send = prep(core.reshape(1).astype(jnp.int32), w)
    block = jnp.minimum(sec * T // 128, 10)
    info = jnp.stack([block, sec * T - block * 128, seq, 15 - seq]).astype(jnp.int32)
    info, send = lax.optimization_barrier((info, send))
    mine = lax.all_to_all(send, "y", 0, 0, tiled=True)
    gain = lax.dynamic_index_in_dim(gains[1].reshape(4, 4, T), y, 1, False).reshape(Q, 1)
    gain = jnp.broadcast_to(gain, (Q, 128))
    block, sq = first(inputs, halo, gains[0:1], w, info)
    block, sq, mine = lax.optimization_barrier((block, sq, mine))
    other = lax.ppermute(mine, "core", [(0, 1), (1, 0)])
    below, above = shift(block, "x", 1), shift(block, "x", -1)
    got = [block, below, above, shift(below[:HB], "x", 1), shift(above[HB:], "x", -1)]
    for axis in ("x", "y"):
        sq = sq + lax.ppermute(sq, axis, [(i, i ^ 1) for i in range(4)])
        sq = sq + lax.ppermute(sq, axis, [(i, i ^ 2) for i in range(4)])
    rel = [x, x + 3, x + 1, x + 2, y, y + 3, y + 1, y + 2]
    order = jnp.concatenate([jnp.stack(rel) % 4, core.reshape(1)]).astype(jnp.int32)
    half = jax.ShapeDtypeStruct((HB, S), jnp.bfloat16)
    full = jax.ShapeDtypeStruct((M * T, S), jnp.bfloat16)
    h, far0, far1 = stage(
        far_kernel,
        order,
        (*got, sq, gain, mine, other),
        [whole(B, S)] * 3 + [whole(HB, S), whole(B - HB, S), whole(1, N), whole(Q, 128)] + picked(7),
        [jax.ShapeDtypeStruct((Q, N), jnp.bfloat16), half, half],
        [pltpu.VMEM((8, N), jnp.float32)],
        4 * R * Q * N,
        "far",
    )
    r0, r1 = shift(far0, "y", 1), shift(far1, "y", -1)
    plus, minus = stage(
        near_kernel,
        order,
        (h, mine, other, mine, other, r0, r1),
        [whole(Q, N)] + picked(6) + picked(5) + [whole(HB, S)] * 2,
        [full, full],
        [],
        4 * R * Q * N,
        "near",
    )
    plus, minus, h = lax.optimization_barrier((plus, minus, h))
    (base,) = stage(
        own_kernel,
        order,
        (h, mine, other, block),
        [whole(Q, N)] + picked(4) + [whole(B, S)],
        [jax.ShapeDtypeStruct((M * T, S), jnp.float32)],
        [],
        2 * R * Q * N,
        "own",
    )
    total = base + shift(plus, "y", 1).astype(jnp.float32) + shift(minus, "y", -1).astype(jnp.float32)
    out = jnp.concatenate([block[: M * T], total.astype(jnp.bfloat16)], 0)
    return out.reshape(2, M, T, S).transpose(0, 1, 3, 2)


def solution(mesh):
    grid = Mesh(mesh.devices.reshape(4, 4, 8, 2), ("x", "y", "z", "core"))
    in_specs = (P(None, ("z", "core"), None), P(None, None, None, ("x", "y")), P())
    out_specs = P(None, None, ("z", "core"), ("x", "y"))
    return jax.shard_map(local, mesh=grid, in_specs=in_specs, out_specs=out_specs, check_vma=False)
```

```python
import functools
import jax
import jax.numpy as jnp
from jax import lax
from jax.experimental import pallas as pl
from jax.experimental.pallas import tpu as pltpu
from jax.sharding import Mesh, PartitionSpec as P

C = 1536
T = 96
R = 480
S = 512
M = 4
B = 400
HB = 192
Q = 384
HR = 240
N = M * S + 128
NT = (((1,), (1,)), ((), ()))


def whole(*shape):
    return pl.BlockSpec(shape, lambda i, *_: (0,) * len(shape))


def gelu(z):
    half = 0.5 * z
    return half + half * jnp.tanh(z * (0.7978845608028654 + 0.035677408136300125 * (z * z)))


def combine(wide):
    n = wide.shape[1]
    total = wide[2 * T : 3 * T]
    for k in (0, 1, 3, 4):
        total = total + pltpu.roll(wide[k * T : (k + 1) * T], (2 - k) % n, 1)
    return total


def first_kernel(info, x_ref, halo_ref, gain_ref, w_ref, o_ref, sq_ref, h_ref, y_ref, hy_ref, hr_ref):
    i = pl.program_id(0)
    start = pl.multiple_of(info[0] * 128, 128)
    off = info[1]
    row = lax.broadcasted_iota(jnp.int32, (T, 256), 0)
    col = lax.broadcasted_iota(jnp.int32, (T, 256), 1)
    pick = jnp.where(col == row + off, 1.0, 0.0).astype(jnp.bfloat16)

    def hidden(v):
        v = v.astype(jnp.float32)
        scale = lax.rsqrt(jnp.sum(v * v, axis=-1, keepdims=True) * (1.0 / C) + 1e-06)
        return gelu(v * scale * gain_ref[...]).astype(jnp.bfloat16)

    @pl.when(i == 0)
    def _():
        hh = hidden(halo_ref[...])
        hy_ref[...] = jnp.zeros_like(hy_ref)
        hr_ref[...] = jnp.zeros_like(hr_ref)
        sq_ref[...] = jnp.zeros_like(sq_ref)
        hy = lax.dot_general(w_ref[...], hh, NT, preferred_element_type=jnp.float32)
        hx = lax.dot_general(pick, halo_ref[:, pl.ds(start, 256)], NT, preferred_element_type=jnp.float32)
        hy_ref[:, 0:32] = hy
        hy_ref[2 * T : 3 * T, 0:32] += hx

    window = pl.ds(start, 256)
    for c in range(2):
        for r in range(c * 256, c * 256 + 256, 16):
            h_ref[r : r + 16, :] = hidden(x_ref[0, r : r + 16, :])
        at = slice(c * 256, c * 256 + 256)
        to = slice(128 + c * 256, 384 + c * 256)
        y_ref[:, to] = lax.dot_general(w_ref[...], h_ref[at, :], NT, preferred_element_type=jnp.float32)
        y_ref[2 * T : 3 * T, to] += lax.dot_general(
            pick, x_ref[0, at, window], NT, preferred_element_type=jnp.float32
        )
    y_ref[:, 0:128] = pltpu.roll(hy_ref[...], lax.rem(252 - 8 * i, 128), 1)
    y_ref[:, 128 + S :] = pltpu.roll(hy_ref[...], lax.rem(252 - 8 * i, 128), 1)
    out = combine(y_ref[...])
    out = out.astype(jnp.bfloat16)
    o_ref[pl.ds(pl.multiple_of(i * T, 16), T), :] = out[:, 128 : 128 + S]
    out = out.astype(jnp.float32)
    squares = jnp.sum(out * out, axis=0, keepdims=True)
    sq_ref[:, pl.ds(pl.multiple_of(i * S, 128), S)] = squares[:, 128 : 128 + S]
    pad = jnp.zeros((32, 128), jnp.float32)
    left = jnp.concatenate([out[:, 0:128], pad], 0).T
    right = jnp.concatenate([out[:, 128 + S :], pad], 0).T
    keep_left = (info[2] > 0).astype(jnp.float32)
    keep_right = (info[3] > 0).astype(jnp.float32)
    lane = lax.broadcasted_iota(jnp.int32, (1, 128), 1) - 4 * i
    turn = lax.rem(4 * i + 2, 128)
    edge = jnp.where((lane == 0) | (lane == 1), pltpu.roll(squares[:, 0:128], turn, 1) * keep_left, 0.0)
    edge += jnp.where((lane == 2) | (lane == 3), pltpu.roll(squares[:, 128 + S :], turn, 1) * keep_right, 0.0)
    sq_ref[:, M * S :] += edge
    line = jnp.concatenate(
        [left[126:127] * keep_left, left[127:128] * keep_left, right[0:1] * keep_right, right[1:2] * keep_right], 1
    )
    hr_ref[pl.ds(i, 1), :] = line
    o_ref[M * T :, :] = hr_ref[...].astype(jnp.bfloat16)


def first(x, halo, gain, w, info):
    return pl.pallas_call(
        first_kernel,
        grid_spec=pltpu.PrefetchScalarGridSpec(
            num_scalar_prefetch=1,
            grid=(M,),
            in_specs=[
                pl.BlockSpec((1, S, C), lambda i, info: (i, 0, 0)),
                whole(32, C),
                whole(1, C),
                pl.BlockSpec((None, R, C), lambda i, info: (0, 0, 0)),
            ],
            out_specs=[whole(B, S), whole(1, N)],
            scratch_shapes=[
                pltpu.VMEM((S, C), jnp.bfloat16),
                pltpu.VMEM((R, S + 256), jnp.float32),
                pltpu.VMEM((R, 128), jnp.float32),
                pltpu.VMEM((16, S), jnp.float32),
            ],
        ),
        out_shape=[jax.ShapeDtypeStruct((B, S), jnp.bfloat16), jax.ShapeDtypeStruct((1, N), jnp.float32)],
        compiler_params=pltpu.CompilerParams(dimension_semantics=("arbitrary",), vmem_limit_bytes=32 << 20),
        cost_estimate=pl.CostEstimate(flops=2 * M * S * R * C, bytes_accessed=2 * M * S * C, transcendentals=M * S * C),
        name="first",
    )(info, x, halo, gain, w)


def prep_kernel(core, w_ref, o_ref):
    for r in range(0, HR, 80):
        v = w_ref[r : r + 80, :].astype(jnp.float32)
        for b in range(4):
            cols = [v[:, (a * 4 + b) * T : (a * 4 + b) * T + T] for a in range(4)]
            o_ref[b, r : r + 80, :] = jnp.concatenate(cols, 1).astype(jnp.bfloat16)


def prep(core, w):
    return pl.pallas_call(
        prep_kernel,
        grid_spec=pltpu.PrefetchScalarGridSpec(
            num_scalar_prefetch=1,
            grid=(1,),
            in_specs=[pl.BlockSpec((None, HR, C), lambda i, core: (1, core[0], 0))],
            out_specs=whole(4, HR, Q),
        ),
        out_shape=jax.ShapeDtypeStruct((4, HR, Q), jnp.bfloat16),
        compiler_params=pltpu.CompilerParams(vmem_limit_bytes=16 << 20),
        cost_estimate=pl.CostEstimate(flops=0, bytes_accessed=4 * HR * C, transcendentals=0),
        name="prep",
    )(core, w)


def join(core, pairs, v_ref):
    for k, (mine_ref, other_ref) in enumerate(pairs):
        v_ref[pl.ds(pl.multiple_of(k * R + core * HR, 16), HR), :] = mine_ref[...]
        v_ref[pl.ds(pl.multiple_of(k * R + HR - core * HR, 16), HR), :] = other_ref[...]


def taps(y_ref, k, j):
    rows = slice(k * R, k * R + R)
    edge = pltpu.roll(y_ref[rows, M * S :], 126 - 4 * j, 1)
    wide = jnp.concatenate([edge, y_ref[rows, j * S : j * S + S], edge], 1)
    return combine(wide)[:, 128 : 128 + S]


def far_kernel(order, a0, a1, a2, a3, a4, sq_ref, gain_ref, wa_ref, wb_ref, h_ref, far0_ref, far1_ref, y_ref, v_ref, s_ref):
    join(order[8], [(wa_ref, wb_ref)], v_ref)
    s_ref[...] = jnp.broadcast_to(lax.rsqrt(sq_ref[...] * (1.0 / C) + 1e-06), s_ref.shape)

    def put(piece, parts, lines):
        dest = pl.multiple_of(order[piece] * T, 16)
        gain = gain_ref[pl.ds(dest, T), :]
        lines = lines.astype(jnp.float32)
        tile = jnp.concatenate(
            [lines[j : j + 1, 128 * q : 128 * q + 128] for j in range(M) for q in range(4)]
            + [jnp.zeros((112, 128), jnp.float32)],
            0,
        )
        h_ref[pl.ds(dest, T), M * S :] = gelu(tile.T[0:T] * s_ref[0:1, M * S :] * gain).astype(jnp.bfloat16)
        for j in range(M):
            ref, row = parts[j]
            for q in range(4):
                lane = slice(j * S + 128 * q, j * S + 128 * q + 128)
                v = ref[row : row + T, 128 * q : 128 * q + 128].astype(jnp.float32)
                h_ref[pl.ds(dest, T), lane] = gelu(v * s_ref[0:1, lane] * gain).astype(jnp.bfloat16)

    for piece, ref in enumerate((a0, a1, a2)):
        put(piece, [(ref, j * T) for j in range(M)], ref[M * T :, :])
    put(3, [(a3, 0), (a3, T), (a4, 0), (a4, T)], a4[HB:, :])
    y_ref[...] = jnp.dot(v_ref[...], h_ref[...], preferred_element_type=jnp.float32)
    for j in range(2):
        far0_ref[j * T : j * T + T, :] = taps(y_ref, 0, j).astype(jnp.bfloat16)
        far1_ref[j * T : j * T + T, :] = taps(y_ref, 0, j + 2).astype(jnp.bfloat16)


def picked(k):
    return [pl.BlockSpec((None, HR, Q), lambda i, order: (order[k], 0, 0))] * 2


def stage(kernel, order, args, in_specs, outs, scratch, count, name):
    return pl.pallas_call(
        kernel,
        grid_spec=pltpu.PrefetchScalarGridSpec(
            num_scalar_prefetch=1,
            grid=(1,),
            in_specs=in_specs,
            out_specs=[whole(*o.shape) for o in outs],
            scratch_shapes=[pltpu.VMEM((count * R, N), jnp.float32), pltpu.VMEM((count * R, Q), jnp.bfloat16)] + scratch,
        ),
        out_shape=outs,
        compiler_params=pltpu.CompilerParams(vmem_limit_bytes=40 << 20),
        cost_estimate=pl.CostEstimate(flops=2 * count * R * Q * N, bytes_accessed=4 * Q * N, transcendentals=0),
        name=name,
    )(order, *args)


def near_kernel(order, h_ref, pa_ref, pb_ref, ma_ref, mb_ref, p_ref, m_ref, y_ref, v_ref):
    join(order[8], [(pa_ref, pb_ref), (ma_ref, mb_ref)], v_ref)
    y_ref[...] = jnp.dot(v_ref[...], h_ref[...], preferred_element_type=jnp.float32)
    for j in range(M):
        p_ref[j * T : j * T + T, :] = taps(y_ref, 0, j)
        m_ref[j * T : j * T + T, :] = taps(y_ref, 1, j)


def own_kernel(order, h_ref, wa_ref, wb_ref, a_ref, o_ref, y_ref, v_ref):
    join(order[8], [(wa_ref, wb_ref)], v_ref)
    y_ref[...] = jnp.dot(v_ref[...], h_ref[...], preferred_element_type=jnp.float32)
    for j in range(M):
        at = slice(j * T, j * T + T)
        o_ref[at, :] = taps(y_ref, 0, j) + a_ref[at, :].astype(jnp.float32)


def shift(value, axis, d):
    return lax.ppermute(value, axis, [(i, (i + d) % 4) for i in range(4)])


def local(inputs, weights, gains):
    x, y, core = lax.axis_index("x"), lax.axis_index("y"), lax.axis_index("core")
    sec = x * 4 + y
    seq = lax.axis_index("z") * 2 + core
    w = pltpu.with_memory_space_constraint(weights.transpose(0, 1, 3, 2).reshape(2, R, C), pltpu.HBM)
    held = pltpu.with_memory_space_constraint(inputs, pltpu.HBM)
    up = [(i, i + 1) for i in range(15)]
    down = [(i + 1, i) for i in range(15)]
    before = lax.ppermute(inputs[:, S - 4 :], ("z", "core"), up)
    after = lax.ppermute(inputs[:, :4], ("z", "core"), down)
    halo = jnp.concatenate([before, after], 1).reshape(32, C)
    send = prep(core.reshape(1).astype(jnp.int32), w)
    block = jnp.minimum(sec * T // 128, 10)
    info = jnp.stack([block, sec * T - block * 128, seq, 15 - seq]).astype(jnp.int32)
    info, send = lax.optimization_barrier((info, send))
    mine = lax.all_to_all(send, "y", 0, 0, tiled=True)
    gain = lax.dynamic_index_in_dim(gains[1].reshape(4, 4, T), y, 1, False).reshape(Q, 1)
    gain = jnp.broadcast_to(gain, (Q, 128))
    block, sq = first(held, halo, gains[0:1], w, info)
    block, sq, mine = lax.optimization_barrier((block, sq, mine))
    other = lax.ppermute(mine, "core", [(0, 1), (1, 0)])
    below, above = shift(block, "x", 1), shift(block, "x", -1)
    got = [block, below, above, shift(below[:HB], "x", 1), shift(above[HB:], "x", -1)]
    for axis in ("y", "x"):
        sq = sq + lax.ppermute(sq, axis, [(i, i ^ 1) for i in range(4)])
        sq = sq + lax.ppermute(sq, axis, [(i, i ^ 2) for i in range(4)])
    rel = [x, x + 3, x + 1, x + 2, y, y + 3, y + 1, y + 2]
    order = jnp.concatenate([jnp.stack(rel) % 4, core.reshape(1)]).astype(jnp.int32)
    half = jax.ShapeDtypeStruct((HB, S), jnp.bfloat16)
    h, far0, far1 = stage(
        far_kernel,
        order,
        (*got, sq, gain, mine, other),
        [whole(B, S)] * 3 + [whole(HB, S), whole(B - HB, S), whole(1, N), whole(Q, 128)] + picked(7),
        [jax.ShapeDtypeStruct((Q, N), jnp.bfloat16), half, half],
        [pltpu.VMEM((8, N), jnp.float32)],
        1,
        "far",
    )
    r0, r1 = shift(far0, "y", 1), shift(far1, "y", -1)
    one = jax.ShapeDtypeStruct((M * T, S), jnp.float32)
    plus, minus = stage(
        near_kernel,
        order,
        (h, mine, other, mine, other),
        [whole(Q, N)] + picked(6) + picked(5),
        [one, one],
        [],
        2,
        "near",
    )
    plus, minus, r0, r1 = lax.optimization_barrier((plus, minus, r0, r1))
    plus = jnp.concatenate([plus[:HB] + r0.astype(jnp.float32), plus[HB:]], 0).astype(jnp.bfloat16)
    minus = jnp.concatenate([minus[:HB], minus[HB:] + r1.astype(jnp.float32)], 0).astype(jnp.bfloat16)
    plus, minus, h = lax.optimization_barrier((plus, minus, h))
    (base,) = stage(
        own_kernel,
        order,
        (h, mine, other, block),
        [whole(Q, N)] + picked(4) + [whole(B, S)],
        [one],
        [],
        1,
        "own",
    )
    total = base + shift(plus, "y", 1).astype(jnp.float32) + shift(minus, "y", -1).astype(jnp.float32)
    out = jnp.concatenate([block[: M * T], total.astype(jnp.bfloat16)], 0)
    return out.reshape(2, M, T, S).transpose(0, 1, 3, 2)


def solution(mesh):
    grid = Mesh(mesh.devices.reshape(4, 4, 8, 2), ("x", "y", "z", "core"))
    in_specs = (P(None, ("z", "core"), None), P(None, None, None, ("x", "y")), P())
    out_specs = P(None, None, ("z", "core"), ("x", "y"))
    return jax.shard_map(local, mesh=grid, in_specs=in_specs, out_specs=out_specs, check_vma=False)
```

```python
import functools
import jax
import jax.numpy as jnp
from jax import lax
from jax.experimental import pallas as pl
from jax.experimental.pallas import tpu as pltpu
from jax.sharding import Mesh, PartitionSpec as P

C = 1536
T = 96
R = 480
S = 512
M = 4
B = 208
HB = 192
L = 17
Q = 384
HR = 240
N = M * S + 128
NT = (((1,), (1,)), ((), ()))


def whole(*shape):
    return pl.BlockSpec(shape, lambda i, *_: (0,) * len(shape))


def gelu(z):
    half = 0.5 * z
    return half + half * jnp.tanh(z * (0.7978845608028654 + 0.035677408136300125 * (z * z)))


def combine(wide):
    n = wide.shape[1]
    total = wide[2 * T : 3 * T]
    for k in (0, 1, 3, 4):
        total = total + pltpu.roll(wide[k * T : (k + 1) * T], (2 - k) % n, 1)
    return total


def first_kernel(info, x_ref, halo_ref, gain_ref, w_ref, o_ref, sq_ref, h_ref, y_ref, hy_ref, hr_ref, base):
    i = pl.program_id(0)
    start = pl.multiple_of(info[0] * 128, 128)
    off = info[1]
    row = lax.broadcasted_iota(jnp.int32, (T, 256), 0)
    col = lax.broadcasted_iota(jnp.int32, (T, 256), 1)
    pick = jnp.where(col == row + off, 1.0, 0.0).astype(jnp.bfloat16)

    def hidden(v):
        v = v.astype(jnp.float32)
        scale = lax.rsqrt(jnp.sum(v * v, axis=-1, keepdims=True) * (1.0 / C) + 1e-06)
        return gelu(v * scale * gain_ref[...]).astype(jnp.bfloat16)

    @pl.when(i == 0)
    def _():
        hh = hidden(halo_ref[...])
        hy_ref[...] = jnp.zeros_like(hy_ref)
        hr_ref[...] = jnp.zeros_like(hr_ref)
        sq_ref[...] = jnp.zeros_like(sq_ref)
        hy = lax.dot_general(w_ref[...], hh, NT, preferred_element_type=jnp.float32)
        hx = lax.dot_general(pick, halo_ref[:, pl.ds(start, 256)], NT, preferred_element_type=jnp.float32)
        hy_ref[:, 0:32] = hy
        hy_ref[2 * T : 3 * T, 0:32] += hx

    window = pl.ds(start, 256)
    for c in range(2):
        for r in range(c * 256, c * 256 + 256, 16):
            h_ref[r : r + 16, :] = hidden(x_ref[0, r : r + 16, :])
        at = slice(c * 256, c * 256 + 256)
        to = slice(128 + c * 256, 384 + c * 256)
        y_ref[:, to] = lax.dot_general(w_ref[...], h_ref[at, :], NT, preferred_element_type=jnp.float32)
        y_ref[2 * T : 3 * T, to] += lax.dot_general(
            pick, x_ref[0, at, window], NT, preferred_element_type=jnp.float32
        )
    b = base + i
    y_ref[:, 0:128] = pltpu.roll(hy_ref[...], lax.rem(252 - 8 * b, 128), 1)
    y_ref[:, 128 + S :] = pltpu.roll(hy_ref[...], lax.rem(252 - 8 * b, 128), 1)
    out = combine(y_ref[...])
    out = out.astype(jnp.bfloat16)
    o_ref[pl.ds(pl.multiple_of(i * T, 16), T), :] = out[:, 128 : 128 + S]
    out = out.astype(jnp.float32)
    squares = jnp.sum(out * out, axis=0, keepdims=True)
    for q in range(4):
        sq_ref[pl.ds(4 * b + q, 1), :] = squares[:, 128 + 128 * q : 256 + 128 * q]
    pad = jnp.zeros((32, 128), jnp.float32)
    left = jnp.concatenate([out[:, 0:128], pad], 0).T
    right = jnp.concatenate([out[:, 128 + S :], pad], 0).T
    keep_left = (info[2] > 0).astype(jnp.float32)
    keep_right = (info[3] > 0).astype(jnp.float32)
    lane = lax.broadcasted_iota(jnp.int32, (1, 128), 1) - 4 * b
    turn = lax.rem(4 * b + 2, 128)
    edge = jnp.where((lane == 0) | (lane == 1), pltpu.roll(squares[:, 0:128], turn, 1) * keep_left, 0.0)
    edge += jnp.where((lane == 2) | (lane == 3), pltpu.roll(squares[:, 128 + S :], turn, 1) * keep_right, 0.0)
    sq_ref[L - 1 : L, :] += edge
    line = jnp.concatenate(
        [left[126:127] * keep_left, left[127:128] * keep_left, right[0:1] * keep_right, right[1:2] * keep_right], 1
    )
    hr_ref[pl.ds(i, 1), :] = line
    o_ref[HB:, :] = hr_ref[...].astype(jnp.bfloat16)


def first(x, halo, gain, w, info, base):
    return pl.pallas_call(
        functools.partial(first_kernel, base=base),
        grid_spec=pltpu.PrefetchScalarGridSpec(
            num_scalar_prefetch=1,
            grid=(2,),
            in_specs=[
                pl.BlockSpec((1, S, C), lambda i, info: (base + i, 0, 0)),
                whole(32, C),
                whole(1, C),
                pl.BlockSpec((None, R, C), lambda i, info: (0, 0, 0)),
            ],
            out_specs=[whole(B, S), whole(L, 128)],
            scratch_shapes=[
                pltpu.VMEM((S, C), jnp.bfloat16),
                pltpu.VMEM((R, S + 256), jnp.float32),
                pltpu.VMEM((R, 128), jnp.float32),
                pltpu.VMEM((16, S), jnp.float32),
            ],
        ),
        out_shape=[jax.ShapeDtypeStruct((B, S), jnp.bfloat16), jax.ShapeDtypeStruct((L, 128), jnp.float32)],
        compiler_params=pltpu.CompilerParams(dimension_semantics=("arbitrary",), vmem_limit_bytes=32 << 20),
        cost_estimate=pl.CostEstimate(flops=4 * S * R * C, bytes_accessed=4 * S * C, transcendentals=2 * S * C),
        name="first",
    )(info, x, halo, gain, w)


def prep_kernel(core, w_ref, o_ref):
    o_ref[...] = w_ref[...]


def prep(core, w):
    return pl.pallas_call(
        prep_kernel,
        grid_spec=pltpu.PrefetchScalarGridSpec(
            num_scalar_prefetch=1,
            grid=(4,),
            in_specs=[pl.BlockSpec((None, HR, Q), lambda i, core: (1, core[0], i))],
            out_specs=pl.BlockSpec((None, HR, Q), lambda i, core: (i, 0, 0)),
        ),
        out_shape=jax.ShapeDtypeStruct((4, HR, Q), jnp.bfloat16),
        cost_estimate=pl.CostEstimate(flops=0, bytes_accessed=4 * HR * C, transcendentals=0),
        name="prep",
    )(core, w)


def join(core, pairs, v_ref):
    for k, (mine_ref, other_ref) in enumerate(pairs):
        v_ref[pl.ds(pl.multiple_of(k * R + core * HR, 16), HR), :] = mine_ref[...]
        v_ref[pl.ds(pl.multiple_of(k * R + HR - core * HR, 16), HR), :] = other_ref[...]


def taps(y_ref, k, j):
    rows = slice(k * R, k * R + R)
    edge = pltpu.roll(y_ref[rows, M * S :], 126 - 4 * j, 1)
    wide = jnp.concatenate([edge, y_ref[rows, j * S : j * S + S], edge], 1)
    return combine(wide)[:, 128 : 128 + S]


def far_kernel(order, *refs):
    got, (sq_ref, gain_ref, wa_ref, wb_ref, h_ref, far0_ref, far1_ref, y_ref, v_ref, s_ref) = refs[:8], refs[8:]
    join(order[8], [(wa_ref, wb_ref)], v_ref)
    total = sq_ref[0]
    for n in range(1, 16):
        total = total + sq_ref[n]
    scale = lax.rsqrt(total * (1.0 / C) + 1e-06)
    for r in range(L):
        s_ref[:, 128 * r : 128 * r + 128] = jnp.broadcast_to(scale[r : r + 1, :], (8, 128))

    for piece in range(4):
        pair = got[2 * piece : 2 * piece + 2]
        dest = pl.multiple_of(order[piece] * T, 16)
        gain = gain_ref[pl.ds(dest, T), :]
        lines = [ref[HB:, :].astype(jnp.float32) for ref in pair]
        tile = jnp.concatenate(
            [lines[j // 2][j % 2 : j % 2 + 1, 128 * q : 128 * q + 128] for j in range(M) for q in range(4)]
            + [jnp.zeros((112, 128), jnp.float32)],
            0,
        )
        h_ref[pl.ds(dest, T), M * S :] = gelu(tile.T[0:T] * s_ref[0:1, M * S :] * gain).astype(jnp.bfloat16)
        for j in range(M):
            row = j % 2 * T
            for q in range(4):
                lane = slice(j * S + 128 * q, j * S + 128 * q + 128)
                v = pair[j // 2][row : row + T, 128 * q : 128 * q + 128].astype(jnp.float32)
                h_ref[pl.ds(dest, T), lane] = gelu(v * s_ref[0:1, lane] * gain).astype(jnp.bfloat16)

    y_ref[...] = jnp.dot(v_ref[...], h_ref[...], preferred_element_type=jnp.float32)
    for j in range(2):
        far0_ref[j * T : j * T + T, :] = taps(y_ref, 0, j).astype(jnp.bfloat16)
        far1_ref[j * T : j * T + T, :] = taps(y_ref, 0, j + 2).astype(jnp.bfloat16)


def picked(k):
    return [pl.BlockSpec((None, HR, Q), lambda i, order: (order[k], 0, 0))] * 2


def stage(kernel, order, args, in_specs, outs, scratch, count, name):
    return pl.pallas_call(
        kernel,
        grid_spec=pltpu.PrefetchScalarGridSpec(
            num_scalar_prefetch=1,
            grid=(1,),
            in_specs=in_specs,
            out_specs=[whole(*o.shape) for o in outs],
            scratch_shapes=[pltpu.VMEM((count * R, N), jnp.float32), pltpu.VMEM((count * R, Q), jnp.bfloat16)] + scratch,
        ),
        out_shape=outs,
        compiler_params=pltpu.CompilerParams(vmem_limit_bytes=40 << 20),
        cost_estimate=pl.CostEstimate(flops=2 * count * R * Q * N, bytes_accessed=4 * Q * N, transcendentals=0),
        name=name,
    )(order, *args)


def near_kernel(order, h_ref, pa_ref, pb_ref, ma_ref, mb_ref, p_ref, m_ref, y_ref, v_ref):
    join(order[8], [(pa_ref, pb_ref), (ma_ref, mb_ref)], v_ref)
    y_ref[...] = jnp.dot(v_ref[...], h_ref[...], preferred_element_type=jnp.float32)
    for j in range(M):
        p_ref[j * T : j * T + T, :] = taps(y_ref, 0, j)
        m_ref[j * T : j * T + T, :] = taps(y_ref, 1, j)


def own_kernel(order, h_ref, wa_ref, wb_ref, a0_ref, a1_ref, o_ref, y_ref, v_ref):
    join(order[8], [(wa_ref, wb_ref)], v_ref)
    y_ref[...] = jnp.dot(v_ref[...], h_ref[...], preferred_element_type=jnp.float32)
    for j in range(M):
        at = slice(j * T, j * T + T)
        a = (a0_ref, a1_ref)[j // 2][j % 2 * T : j % 2 * T + T, :]
        o_ref[at, :] = taps(y_ref, 0, j) + a.astype(jnp.float32)


def shift(value, axis, d):
    return lax.ppermute(value, axis, [(i, (i + d) % 4) for i in range(4)])


def local(inputs, weights, gains):
    x, y, core = lax.axis_index("x"), lax.axis_index("y"), lax.axis_index("core")
    sec = x * 4 + y
    seq = lax.axis_index("z") * 2 + core
    w = pltpu.with_memory_space_constraint(weights.transpose(0, 1, 3, 2).reshape(2, R, C), pltpu.HBM)
    held = pltpu.with_memory_space_constraint(inputs, pltpu.HBM)
    up = [(i, i + 1) for i in range(15)]
    down = [(i + 1, i) for i in range(15)]
    before = lax.ppermute(inputs[:, S - 4 :], ("z", "core"), up)
    after = lax.ppermute(inputs[:, :4], ("z", "core"), down)
    halo = jnp.concatenate([before, after], 1).reshape(32, C)
    send = prep(core.reshape(1).astype(jnp.int32), w)
    block = jnp.minimum(sec * T // 128, 10)
    info = jnp.stack([block, sec * T - block * 128, seq, 15 - seq]).astype(jnp.int32)
    info, send = lax.optimization_barrier((info, send))
    mine = lax.all_to_all(send, "x", 0, 0, tiled=True)
    gain = lax.dynamic_index_in_dim(gains[1].reshape(4, Q), x, 0, False).reshape(Q, 1)
    gain = jnp.broadcast_to(gain, (Q, 128))
    one0, sq0 = first(held, halo, gains[0:1], w, info, 0)
    one1, sq1 = first(held, halo, gains[0:1], w, info, 2)
    one1, sq1, mine = lax.optimization_barrier((one1, sq1, mine))
    below0, above0 = shift(one0, "y", 1), shift(one0, "y", -1)
    below1, above1 = shift(one1, "y", 1), shift(one1, "y", -1)
    got = [one0, one1, below0, below1, above0, above1, shift(below0, "y", 1), shift(above1, "y", -1)]
    sq = jnp.broadcast_to((sq0 + sq1)[None], (16, L, 128))
    sq = lax.all_to_all(sq, ("x", "y"), 0, 0, tiled=True)
    other = lax.ppermute(mine, "core", [(0, 1), (1, 0)])
    rel = [y, y + 3, y + 1, y + 2, x, x + 3, x + 1, x + 2]
    order = jnp.concatenate([jnp.stack(rel) % 4, core.reshape(1)]).astype(jnp.int32)
    half = jax.ShapeDtypeStruct((HB, S), jnp.bfloat16)
    h, far0, far1 = stage(
        far_kernel,
        order,
        (*got, sq, gain, mine, other),
        [whole(B, S)] * 8 + [whole(16, L, 128), whole(Q, 128)] + picked(7),
        [jax.ShapeDtypeStruct((Q, N), jnp.bfloat16), half, half],
        [pltpu.VMEM((8, N), jnp.float32)],
        1,
        "far",
    )
    r0, r1 = shift(far0, "x", 1), shift(far1, "x", -1)
    wide = jax.ShapeDtypeStruct((M * T, S), jnp.float32)
    plus, minus = stage(
        near_kernel,
        order,
        (h, mine, other, mine, other),
        [whole(Q, N)] + picked(6) + picked(5),
        [wide, wide],
        [],
        2,
        "near",
    )
    plus, minus, r0, r1 = lax.optimization_barrier((plus, minus, r0, r1))
    plus = jnp.concatenate([plus[:HB] + r0.astype(jnp.float32), plus[HB:]], 0).astype(jnp.bfloat16)
    minus = jnp.concatenate([minus[:HB], minus[HB:] + r1.astype(jnp.float32)], 0).astype(jnp.bfloat16)
    plus, minus, h = lax.optimization_barrier((plus, minus, h))
    (base,) = stage(
        own_kernel,
        order,
        (h, mine, other, one0, one1),
        [whole(Q, N)] + picked(4) + [whole(B, S)] * 2,
        [wide],
        [],
        1,
        "own",
    )
    total = base + shift(plus, "x", 1).astype(jnp.float32) + shift(minus, "x", -1).astype(jnp.float32)
    out = jnp.concatenate([one0[:HB], one1[:HB], total.astype(jnp.bfloat16)], 0)
    return out.reshape(2, M, T, S).transpose(0, 1, 3, 2)


def solution(mesh):
    grid = Mesh(mesh.devices.reshape(4, 4, 8, 2), ("x", "y", "z", "core"))
    in_specs = (P(None, ("z", "core"), None), P(None, None, None, ("x", "y")), P())
    out_specs = P(None, None, ("z", "core"), ("x", "y"))
    return jax.shard_map(local, mesh=grid, in_specs=in_specs, out_specs=out_specs, check_vma=False)
```

```python
import functools
import jax
import jax.numpy as jnp
from jax import lax
from jax.experimental import pallas as pl
from jax.experimental.pallas import tpu as pltpu
from jax.sharding import Mesh, PartitionSpec as P

C = 1536
T = 96
R = 480
S = 512
M = 4
B = 400
HB = 192
L = 17
Q = 384
HR = 240
N = M * S + 128
NT = (((1,), (1,)), ((), ()))


def whole(*shape):
    return pl.BlockSpec(shape, lambda i, *_: (0,) * len(shape))


def gelu(z):
    half = 0.5 * z
    return half + half * jnp.tanh(z * (0.7978845608028654 + 0.035677408136300125 * (z * z)))


def combine(wide):
    n = wide.shape[1]
    total = wide[2 * T : 3 * T]
    for k in (0, 1, 3, 4):
        total = total + pltpu.roll(wide[k * T : (k + 1) * T], (2 - k) % n, 1)
    return total


def first_kernel(info, x_ref, up_ref, down_ref, gain_ref, w_ref, o_ref, sq_ref, h_ref, y_ref, hy_ref, hr_ref):
    i = pl.program_id(0)
    start = pl.multiple_of(info[0] * 128, 128)
    off = info[1]
    row = lax.broadcasted_iota(jnp.int32, (T, 256), 0)
    col = lax.broadcasted_iota(jnp.int32, (T, 256), 1)
    pick = jnp.where(col == row + off, 1.0, 0.0).astype(jnp.bfloat16)

    def hidden(v):
        v = v.astype(jnp.float32)
        scale = lax.rsqrt(jnp.sum(v * v, axis=-1, keepdims=True) * (1.0 / C) + 1e-06)
        return gelu(v * scale * gain_ref[...]).astype(jnp.bfloat16)

    @pl.when(i == 0)
    def _():
        hr_ref[...] = jnp.zeros_like(hr_ref)
        sq_ref[...] = jnp.zeros_like(sq_ref)
        hy_ref[...] = jnp.zeros_like(hy_ref)
        for n, ref in enumerate((up_ref, down_ref)):
            at = slice(32 * n, 32 * n + 32)
            hy_ref[:, at] = lax.dot_general(w_ref[...], hidden(ref[...]), NT, preferred_element_type=jnp.float32)
            hy_ref[2 * T : 3 * T, at] += lax.dot_general(
                pick, ref[:, pl.ds(start, 256)], NT, preferred_element_type=jnp.float32
            )

    window = pl.ds(start, 256)
    for c in range(2):
        for r in range(c * 256, c * 256 + 256, 16):
            h_ref[r : r + 16, :] = hidden(x_ref[0, r : r + 16, :])
        at = slice(c * 256, c * 256 + 256)
        to = slice(128 + c * 256, 384 + c * 256)
        y_ref[:, to] = lax.dot_general(w_ref[...], h_ref[at, :], NT, preferred_element_type=jnp.float32)
        y_ref[2 * T : 3 * T, to] += lax.dot_general(
            pick, x_ref[0, at, window], NT, preferred_element_type=jnp.float32
        )
    y_ref[:, 0:128] = pltpu.roll(hy_ref[...], 120 - 8 * i, 1)
    y_ref[:, 128 + S :] = pltpu.roll(hy_ref[...], 96 - 8 * i, 1)
    out = combine(y_ref[...])
    out = out.astype(jnp.bfloat16)
    o_ref[pl.ds(pl.multiple_of(i * T, 16), T), :] = out[:, 128 : 128 + S]
    out = out.astype(jnp.float32)
    squares = jnp.sum(out * out, axis=0, keepdims=True)
    for q in range(4):
        sq_ref[pl.ds(4 * i + q, 1), :] = squares[:, 128 + 128 * q : 256 + 128 * q]
    pad = jnp.zeros((32, 128), jnp.float32)
    left = jnp.concatenate([out[:, 0:128], pad], 0).T
    right = jnp.concatenate([out[:, 128 + S :], pad], 0).T
    keep_left = (info[2] > 0).astype(jnp.float32)
    keep_right = (info[3] > 0).astype(jnp.float32)
    lane = lax.broadcasted_iota(jnp.int32, (1, 128), 1) - 4 * i
    turn = lax.rem(4 * i + 2, 128)
    edge = jnp.where((lane == 0) | (lane == 1), pltpu.roll(squares[:, 0:128], turn, 1) * keep_left, 0.0)
    edge += jnp.where((lane == 2) | (lane == 3), pltpu.roll(squares[:, 128 + S :], turn, 1) * keep_right, 0.0)
    sq_ref[L - 1 : L, :] += edge
    line = jnp.concatenate(
        [left[126:127] * keep_left, left[127:128] * keep_left, right[0:1] * keep_right, right[1:2] * keep_right], 1
    )
    hr_ref[pl.ds(i, 1), :] = line
    o_ref[M * T :, :] = hr_ref[...].astype(jnp.bfloat16)


def first(x, up, down, gain, w, info):
    outs = [jax.ShapeDtypeStruct((B, S), jnp.bfloat16), jax.ShapeDtypeStruct((L, 128), jnp.float32)]
    return pl.pallas_call(
        first_kernel,
        grid_spec=pltpu.PrefetchScalarGridSpec(
            num_scalar_prefetch=1,
            grid=(M,),
            in_specs=[
                pl.BlockSpec((1, S, C), lambda i, info: (i, 0, 0)),
                whole(32, C),
                whole(32, C),
                whole(1, C),
                pl.BlockSpec((None, R, C), lambda i, info: (0, 0, 0)),
            ],
            out_specs=[whole(*o.shape) for o in outs],
            scratch_shapes=[
                pltpu.VMEM((S, C), jnp.bfloat16),
                pltpu.VMEM((R, S + 256), jnp.float32),
                pltpu.VMEM((R, 128), jnp.float32),
                pltpu.VMEM((16, S), jnp.float32),
            ],
        ),
        out_shape=outs,
        compiler_params=pltpu.CompilerParams(dimension_semantics=("arbitrary",), vmem_limit_bytes=32 << 20),
        cost_estimate=pl.CostEstimate(flops=2 * M * S * R * C, bytes_accessed=2 * M * S * C, transcendentals=M * S * C),
        name="first",
    )(info, x, up, down, gain, w)


def prep_kernel(core, w_ref, top_ref, end_ref, o_ref, down_ref, up_ref):
    for b in range(4):
        o_ref[b] = w_ref[:, b * Q : b * Q + Q]
        down_ref[b * 8 : b * 8 + 8, :] = top_ref[b]
        up_ref[b * 8 : b * 8 + 8, :] = end_ref[b]


def prep(core, w, x):
    outs = [jax.ShapeDtypeStruct((4, HR, Q), jnp.bfloat16)] + [jax.ShapeDtypeStruct((32, C), jnp.bfloat16)] * 2
    return pl.pallas_call(
        prep_kernel,
        grid_spec=pltpu.PrefetchScalarGridSpec(
            num_scalar_prefetch=1,
            grid=(1,),
            in_specs=[
                pl.BlockSpec((None, HR, C), lambda i, core: (1, core[0], 0)),
                pl.BlockSpec((M, 8, C), lambda i, core: (0, 0, 0)),
                pl.BlockSpec((M, 8, C), lambda i, core: (0, S // 8 - 1, 0)),
            ],
            out_specs=[whole(*o.shape) for o in outs],
        ),
        out_shape=outs,
        cost_estimate=pl.CostEstimate(flops=0, bytes_accessed=4 * HR * C, transcendentals=0),
        name="prep",
    )(core, w, x, x)


def join(core, pairs, v_ref):
    for k, (mine_ref, other_ref) in enumerate(pairs):
        v_ref[pl.ds(pl.multiple_of(k * R + core * HR, 16), HR), :] = mine_ref[...]
        v_ref[pl.ds(pl.multiple_of(k * R + HR - core * HR, 16), HR), :] = other_ref[...]


def taps(y_ref, k, j):
    rows = slice(k * R, k * R + R)
    edge = pltpu.roll(y_ref[rows, M * S :], 126 - 4 * j, 1)
    wide = jnp.concatenate([edge, y_ref[rows, j * S : j * S + S], edge], 1)
    return combine(wide)[:, 128 : 128 + S]


def far_kernel(order, *refs):
    got, (sq_ref, gain_ref, wa_ref, wb_ref, h_ref, far0_ref, far1_ref, y_ref, v_ref, s_ref) = refs[:5], refs[5:]
    join(order[8], [(wa_ref, wb_ref)], v_ref)
    total = sq_ref[...]
    scale = lax.rsqrt(total * (1.0 / C) + 1e-06)
    for r in range(L):
        s_ref[:, 128 * r : 128 * r + 128] = jnp.broadcast_to(scale[r : r + 1, :], (8, 128))

    for piece in range(4):
        if piece < 3:
            parts, lines = [(got[piece], j * T) for j in range(M)], got[piece][M * T :, :]
        else:
            parts, lines = [(got[3 + j // 2], j % 2 * T) for j in range(M)], got[4][HB:, :]
        dest = pl.multiple_of(order[piece] * T, 16)
        gain = gain_ref[pl.ds(dest, T), :]
        lines = lines.astype(jnp.float32)
        tile = jnp.concatenate(
            [lines[j : j + 1, 128 * q : 128 * q + 128] for j in range(M) for q in range(4)]
            + [jnp.zeros((112, 128), jnp.float32)],
            0,
        )
        h_ref[pl.ds(dest, T), M * S :] = gelu(tile.T[0:T] * s_ref[0:1, M * S :] * gain).astype(jnp.bfloat16)
        for j in range(M):
            ref, row = parts[j]
            for q in range(4):
                lane = slice(j * S + 128 * q, j * S + 128 * q + 128)
                v = ref[row : row + T, 128 * q : 128 * q + 128].astype(jnp.float32)
                h_ref[pl.ds(dest, T), lane] = gelu(v * s_ref[0:1, lane] * gain).astype(jnp.bfloat16)

    y_ref[...] = jnp.dot(v_ref[...], h_ref[...], preferred_element_type=jnp.float32)
    for j in range(2):
        far0_ref[j * T : j * T + T, :] = taps(y_ref, 0, j).astype(jnp.bfloat16)
        far1_ref[j * T : j * T + T, :] = taps(y_ref, 0, j + 2).astype(jnp.bfloat16)


def picked(k):
    return [pl.BlockSpec((None, HR, Q), lambda i, order: (order[k], 0, 0))] * 2


def stage(kernel, order, args, in_specs, outs, scratch, count, name):
    return pl.pallas_call(
        kernel,
        grid_spec=pltpu.PrefetchScalarGridSpec(
            num_scalar_prefetch=1,
            grid=(1,),
            in_specs=in_specs,
            out_specs=[whole(*o.shape) for o in outs],
            scratch_shapes=[pltpu.VMEM((count * R, N), jnp.float32), pltpu.VMEM((count * R, Q), jnp.bfloat16)] + scratch,
        ),
        out_shape=outs,
        compiler_params=pltpu.CompilerParams(vmem_limit_bytes=40 << 20),
        cost_estimate=pl.CostEstimate(flops=2 * count * R * Q * N, bytes_accessed=4 * Q * N, transcendentals=0),
        name=name,
    )(order, *args)


def near_kernel(order, h_ref, pa_ref, pb_ref, ma_ref, mb_ref, p_ref, m_ref, y_ref, v_ref):
    join(order[8], [(pa_ref, pb_ref), (ma_ref, mb_ref)], v_ref)
    y_ref[...] = jnp.dot(v_ref[...], h_ref[...], preferred_element_type=jnp.float32)
    for j in range(M):
        p_ref[j * T : j * T + T, :] = taps(y_ref, 0, j)
        m_ref[j * T : j * T + T, :] = taps(y_ref, 1, j)


def own_kernel(order, h_ref, wa_ref, wb_ref, a_ref, o_ref, y_ref, v_ref):
    join(order[8], [(wa_ref, wb_ref)], v_ref)
    y_ref[...] = jnp.dot(v_ref[...], h_ref[...], preferred_element_type=jnp.float32)
    for j in range(M):
        at = slice(j * T, j * T + T)
        o_ref[at, :] = taps(y_ref, 0, j) + a_ref[at, :].astype(jnp.float32)


def shift(value, axis, d):
    return lax.ppermute(value, axis, [(i, (i + d) % 4) for i in range(4)])


def local(inputs, weights, gains):
    x, y, core = lax.axis_index("x"), lax.axis_index("y"), lax.axis_index("core")
    sec = x * 4 + y
    seq = lax.axis_index("z") * 2 + core
    w = pltpu.with_memory_space_constraint(weights.transpose(0, 1, 3, 2).reshape(2, R, C), pltpu.HBM)
    held = pltpu.with_memory_space_constraint(inputs, pltpu.HBM)
    up = [(i, i + 1) for i in range(15)]
    down = [(i + 1, i) for i in range(15)]
    send, top, end = prep(core.reshape(1).astype(jnp.int32), w, held)
    up = lax.ppermute(end, ("z", "core"), up)
    down = lax.ppermute(top, ("z", "core"), down)
    block = jnp.minimum(sec * T // 128, 10)
    info = jnp.stack([block, sec * T - block * 128, seq, 15 - seq]).astype(jnp.int32)
    info, send = lax.optimization_barrier((info, send))
    mine = lax.all_to_all(send, "x", 0, 0, tiled=True)
    gain = lax.dynamic_index_in_dim(gains[1].reshape(4, Q), x, 0, False).reshape(Q, 1)
    gain = jnp.broadcast_to(gain, (Q, 128))
    block, sq = first(held, up, down, gains[0:1], w, info)
    block, sq, mine = lax.optimization_barrier((block, sq, mine))
    below, above = shift(block, "y", 1), shift(block, "y", -1)
    sq = sq + shift(sq, "x", 1) + shift(sq, "x", -1) + shift(sq, "x", 2)
    sq = sq + shift(sq, "y", 1) + shift(sq, "y", -1) + shift(sq, "y", 2)
    swap, below, above, sq = lax.optimization_barrier((mine, below, above, sq))
    other = lax.ppermute(swap, "core", [(0, 1), (1, 0)])
    got = [block, below, above, shift(below[:HB], "y", 1), shift(above[HB:], "y", -1)]
    rel = [y, y + 3, y + 1, y + 2, x, x + 3, x + 1, x + 2]
    order = jnp.concatenate([jnp.stack(rel) % 4, core.reshape(1)]).astype(jnp.int32)
    half = jax.ShapeDtypeStruct((HB, S), jnp.bfloat16)
    h, far0, far1 = stage(
        far_kernel,
        order,
        (*got, sq, gain, mine, other),
        [whole(B, S)] * 3 + [whole(HB, S), whole(B - HB, S), whole(L, 128), whole(Q, 128)] + picked(7),
        [jax.ShapeDtypeStruct((Q, N), jnp.bfloat16), half, half],
        [pltpu.VMEM((8, N), jnp.float32)],
        1,
        "far",
    )
    r0, r1 = shift(far0, "x", 1), shift(far1, "x", -1)
    wide = jax.ShapeDtypeStruct((M * T, S), jnp.float32)
    plus, minus = stage(
        near_kernel,
        order,
        (h, mine, other, mine, other),
        [whole(Q, N)] + picked(6) + picked(5),
        [wide, wide],
        [],
        2,
        "near",
    )
    plus, minus, r0, r1 = lax.optimization_barrier((plus, minus, r0, r1))
    plus = jnp.concatenate([plus[:HB] + r0.astype(jnp.float32), plus[HB:]], 0).astype(jnp.bfloat16)
    minus = jnp.concatenate([minus[:HB], minus[HB:] + r1.astype(jnp.float32)], 0).astype(jnp.bfloat16)
    plus, minus, h = lax.optimization_barrier((plus, minus, h))
    (base,) = stage(
        own_kernel,
        order,
        (h, mine, other, block),
        [whole(Q, N)] + picked(4) + [whole(B, S)],
        [wide],
        [],
        1,
        "own",
    )
    total = base + shift(plus, "x", 1).astype(jnp.float32) + shift(minus, "x", -1).astype(jnp.float32)
    out = jnp.concatenate([block[: M * T], total.astype(jnp.bfloat16)], 0)
    return out.reshape(2, M, T, S).transpose(0, 1, 3, 2)


def solution(mesh):
    grid = Mesh(mesh.devices.reshape(4, 4, 8, 2), ("x", "y", "z", "core"))
    in_specs = (P(None, ("z", "core"), None), P(None, None, None, ("x", "y")), P())
    out_specs = P(None, None, ("z", "core"), ("x", "y"))
    return jax.shard_map(local, mesh=grid, in_specs=in_specs, out_specs=out_specs, check_vma=False)
```

```python
import functools
import jax
import jax.numpy as jnp
from jax import lax
from jax.experimental import pallas as pl
from jax.experimental.pallas import tpu as pltpu
from jax.sharding import Mesh, PartitionSpec as P

C = 1536
T = 96
R = 480
S = 512
M = 4
B = 400
HB = 192
Q = 384
HR = 240
N = M * S + 128
NT = (((1,), (1,)), ((), ()))


def whole(*shape):
    return pl.BlockSpec(shape, lambda i, *_: (0,) * len(shape))


def gelu(z):
    half = 0.5 * z
    return half + half * jnp.tanh(z * (0.7978845608028654 + 0.035677408136300125 * (z * z)))


def combine(wide):
    n = wide.shape[1]
    total = wide[2 * T : 3 * T]
    for k in (0, 1, 3, 4):
        total = total + pltpu.roll(wide[k * T : (k + 1) * T], (2 - k) % n, 1)
    return total


def first_kernel(info, x_ref, halo_ref, gain_ref, w_ref, o_ref, sq_ref, h_ref, y_ref, hy_ref, hr_ref):
    i = pl.program_id(0)
    start = pl.multiple_of(info[0] * 128, 128)
    off = info[1]
    row = lax.broadcasted_iota(jnp.int32, (T, 256), 0)
    col = lax.broadcasted_iota(jnp.int32, (T, 256), 1)
    pick = jnp.where(col == row + off, 1.0, 0.0).astype(jnp.bfloat16)

    def hidden(v):
        v = v.astype(jnp.float32)
        scale = lax.rsqrt(jnp.sum(v * v, axis=-1, keepdims=True) * (1.0 / C) + 1e-06)
        return gelu(v * scale * gain_ref[...]).astype(jnp.bfloat16)

    @pl.when(i == 0)
    def _():
        hh = hidden(halo_ref[...])
        hy_ref[...] = jnp.zeros_like(hy_ref)
        hr_ref[...] = jnp.zeros_like(hr_ref)
        sq_ref[...] = jnp.zeros_like(sq_ref)
        hy = lax.dot_general(w_ref[...], hh, NT, preferred_element_type=jnp.float32)
        hx = lax.dot_general(pick, halo_ref[:, pl.ds(start, 256)], NT, preferred_element_type=jnp.float32)
        hy_ref[:, 0:32] = hy
        hy_ref[2 * T : 3 * T, 0:32] += hx

    window = pl.ds(start, 256)
    for c in range(2):
        for r in range(c * 256, c * 256 + 256, 16):
            h_ref[r : r + 16, :] = hidden(x_ref[0, r : r + 16, :])
        at = slice(c * 256, c * 256 + 256)
        to = slice(128 + c * 256, 384 + c * 256)
        y_ref[:, to] = lax.dot_general(w_ref[...], h_ref[at, :], NT, preferred_element_type=jnp.float32)
        y_ref[2 * T : 3 * T, to] += lax.dot_general(
            pick, x_ref[0, at, window], NT, preferred_element_type=jnp.float32
        )
    y_ref[:, 0:128] = pltpu.roll(hy_ref[...], lax.rem(252 - 8 * i, 128), 1)
    y_ref[:, 128 + S :] = pltpu.roll(hy_ref[...], lax.rem(252 - 8 * i, 128), 1)
    out = combine(y_ref[...])
    out = out.astype(jnp.bfloat16)
    o_ref[pl.ds(pl.multiple_of(i * T, 16), T), :] = out[:, 128 : 128 + S]
    out = out.astype(jnp.float32)
    squares = jnp.sum(out * out, axis=0, keepdims=True)
    sq_ref[:, pl.ds(pl.multiple_of(i * S, 128), S)] = squares[:, 128 : 128 + S]
    pad = jnp.zeros((32, 128), jnp.float32)
    left = jnp.concatenate([out[:, 0:128], pad], 0).T
    right = jnp.concatenate([out[:, 128 + S :], pad], 0).T
    keep_left = (info[2] > 0).astype(jnp.float32)
    keep_right = (info[3] > 0).astype(jnp.float32)
    lane = lax.broadcasted_iota(jnp.int32, (1, 128), 1) - 4 * i
    turn = lax.rem(4 * i + 2, 128)
    edge = jnp.where((lane == 0) | (lane == 1), pltpu.roll(squares[:, 0:128], turn, 1) * keep_left, 0.0)
    edge += jnp.where((lane == 2) | (lane == 3), pltpu.roll(squares[:, 128 + S :], turn, 1) * keep_right, 0.0)
    sq_ref[:, M * S :] += edge
    line = jnp.concatenate(
        [left[126:127] * keep_left, left[127:128] * keep_left, right[0:1] * keep_right, right[1:2] * keep_right], 1
    )
    hr_ref[pl.ds(i, 1), :] = line
    o_ref[M * T :, :] = hr_ref[...].astype(jnp.bfloat16)


def first(x, halo, gain, w, info):
    return pl.pallas_call(
        first_kernel,
        grid_spec=pltpu.PrefetchScalarGridSpec(
            num_scalar_prefetch=1,
            grid=(M,),
            in_specs=[
                pl.BlockSpec((1, S, C), lambda i, info: (i, 0, 0)),
                whole(32, C),
                whole(1, C),
                pl.BlockSpec((None, R, C), lambda i, info: (0, 0, 0)),
            ],
            out_specs=[whole(B, S), whole(1, N)],
            scratch_shapes=[
                pltpu.VMEM((S, C), jnp.bfloat16),
                pltpu.VMEM((R, S + 256), jnp.float32),
                pltpu.VMEM((R, 128), jnp.float32),
                pltpu.VMEM((16, S), jnp.float32),
            ],
        ),
        out_shape=[jax.ShapeDtypeStruct((B, S), jnp.bfloat16), jax.ShapeDtypeStruct((1, N), jnp.float32)],
        compiler_params=pltpu.CompilerParams(dimension_semantics=("arbitrary",), vmem_limit_bytes=32 << 20),
        cost_estimate=pl.CostEstimate(flops=2 * M * S * R * C, bytes_accessed=2 * M * S * C, transcendentals=M * S * C),
        name="first",
    )(info, x, halo, gain, w)


def prep_kernel(core, w_ref, o_ref):
    for r in range(0, HR, 80):
        v = w_ref[r : r + 80, :].astype(jnp.float32)
        for b in range(4):
            cols = [v[:, (a * 4 + b) * T : (a * 4 + b) * T + T] for a in range(4)]
            o_ref[b, r : r + 80, :] = jnp.concatenate(cols, 1).astype(jnp.bfloat16)


def prep(core, w):
    return pl.pallas_call(
        prep_kernel,
        grid_spec=pltpu.PrefetchScalarGridSpec(
            num_scalar_prefetch=1,
            grid=(1,),
            in_specs=[pl.BlockSpec((None, HR, C), lambda i, core: (1, core[0], 0))],
            out_specs=whole(4, HR, Q),
        ),
        out_shape=jax.ShapeDtypeStruct((4, HR, Q), jnp.bfloat16),
        compiler_params=pltpu.CompilerParams(vmem_limit_bytes=16 << 20),
        cost_estimate=pl.CostEstimate(flops=0, bytes_accessed=4 * HR * C, transcendentals=0),
        name="prep",
    )(core, w)


def join(core, pairs, v_ref):
    for k, (mine_ref, other_ref) in enumerate(pairs):
        v_ref[pl.ds(pl.multiple_of(k * R + core * HR, 16), HR), :] = mine_ref[...]
        v_ref[pl.ds(pl.multiple_of(k * R + HR - core * HR, 16), HR), :] = other_ref[...]


def taps(y_ref, k, j):
    rows = slice(k * R, k * R + R)
    edge = pltpu.roll(y_ref[rows, M * S :], 126 - 4 * j, 1)
    wide = jnp.concatenate([edge, y_ref[rows, j * S : j * S + S], edge], 1)
    return combine(wide)[:, 128 : 128 + S]


def far_kernel(order, a0, a1, a2, a3, a4, sq_ref, gain_ref, wa_ref, wb_ref, h_ref, far0_ref, far1_ref, y_ref, v_ref, s_ref):
    join(order[8], [(wa_ref, wb_ref)], v_ref)
    s_ref[...] = jnp.broadcast_to(lax.rsqrt(sq_ref[...] * (1.0 / C) + 1e-06), s_ref.shape)

    def put(piece, parts, lines):
        dest = pl.multiple_of(order[piece] * T, 16)
        gain = gain_ref[pl.ds(dest, T), :]
        lines = lines.astype(jnp.float32)
        tile = jnp.concatenate(
            [lines[j : j + 1, 128 * q : 128 * q + 128] for j in range(M) for q in range(4)]
            + [jnp.zeros((112, 128), jnp.float32)],
            0,
        )
        h_ref[pl.ds(dest, T), M * S :] = gelu(tile.T[0:T] * s_ref[0:1, M * S :] * gain).astype(jnp.bfloat16)
        for j in range(M):
            ref, row = parts[j]
            for q in range(4):
                lane = slice(j * S + 128 * q, j * S + 128 * q + 128)
                v = ref[row : row + T, 128 * q : 128 * q + 128].astype(jnp.float32)
                h_ref[pl.ds(dest, T), lane] = gelu(v * s_ref[0:1, lane] * gain).astype(jnp.bfloat16)

    for piece, ref in enumerate((a0, a1, a2)):
        put(piece, [(ref, j * T) for j in range(M)], ref[M * T :, :])
    put(3, [(a3, 0), (a3, T), (a4, 0), (a4, T)], a4[HB:, :])
    y_ref[...] = jnp.dot(v_ref[...], h_ref[...], preferred_element_type=jnp.float32)
    for j in range(2):
        far0_ref[j * T : j * T + T, :] = taps(y_ref, 0, j).astype(jnp.bfloat16)
        far1_ref[j * T : j * T + T, :] = taps(y_ref, 0, j + 2).astype(jnp.bfloat16)


def picked(k):
    return [pl.BlockSpec((None, HR, Q), lambda i, order: (order[k], 0, 0))] * 2


def stage(kernel, order, args, in_specs, outs, scratch, count, name):
    return pl.pallas_call(
        kernel,
        grid_spec=pltpu.PrefetchScalarGridSpec(
            num_scalar_prefetch=1,
            grid=(1,),
            in_specs=in_specs,
            out_specs=[whole(*o.shape) for o in outs],
            scratch_shapes=[pltpu.VMEM((count * R, N), jnp.float32), pltpu.VMEM((count * R, Q), jnp.bfloat16)] + scratch,
        ),
        out_shape=outs,
        compiler_params=pltpu.CompilerParams(vmem_limit_bytes=40 << 20),
        cost_estimate=pl.CostEstimate(flops=2 * count * R * Q * N, bytes_accessed=4 * Q * N, transcendentals=0),
        name=name,
    )(order, *args)


def near_kernel(order, h_ref, pa_ref, pb_ref, ma_ref, mb_ref, p_ref, m_ref, y_ref, v_ref):
    join(order[8], [(pa_ref, pb_ref), (ma_ref, mb_ref)], v_ref)
    y_ref[...] = jnp.dot(v_ref[...], h_ref[...], preferred_element_type=jnp.float32)
    for j in range(M):
        p_ref[j * T : j * T + T, :] = taps(y_ref, 0, j)
        m_ref[j * T : j * T + T, :] = taps(y_ref, 1, j)


def own_kernel(order, h_ref, wa_ref, wb_ref, a_ref, o_ref, y_ref, v_ref):
    join(order[8], [(wa_ref, wb_ref)], v_ref)
    y_ref[...] = jnp.dot(v_ref[...], h_ref[...], preferred_element_type=jnp.float32)
    for j in range(M):
        at = slice(j * T, j * T + T)
        o_ref[at, :] = taps(y_ref, 0, j) + a_ref[at, :].astype(jnp.float32)


def shift(value, axis, d):
    return lax.ppermute(value, axis, [(i, (i + d) % 4) for i in range(4)])


def local(inputs, weights, gains):
    x, y, core = lax.axis_index("x"), lax.axis_index("y"), lax.axis_index("core")
    sec = x * 4 + y
    seq = lax.axis_index("z") * 2 + core
    w = pltpu.with_memory_space_constraint(weights.transpose(0, 1, 3, 2).reshape(2, R, C), pltpu.HBM)
    held = pltpu.with_memory_space_constraint(inputs, pltpu.HBM)
    up = [(i, i + 1) for i in range(15)]
    down = [(i + 1, i) for i in range(15)]
    before = lax.ppermute(inputs[:, S - 4 :], ("z", "core"), up)
    after = lax.ppermute(inputs[:, :4], ("z", "core"), down)
    halo = jnp.concatenate([before, after], 1).reshape(32, C)
    send = prep(core.reshape(1).astype(jnp.int32), w)
    block = jnp.minimum(sec * T // 128, 10)
    info = jnp.stack([block, sec * T - block * 128, seq, 15 - seq]).astype(jnp.int32)
    info, send = lax.optimization_barrier((info, send))
    mine = lax.all_to_all(send, "y", 0, 0, tiled=True)
    gain = lax.dynamic_index_in_dim(gains[1].reshape(4, 4, T), y, 1, False).reshape(Q, 1)
    gain = jnp.broadcast_to(gain, (Q, 128))
    block, sq = first(held, halo, gains[0:1], w, info)
    block, sq, mine = lax.optimization_barrier((block, sq, mine))
    below, above = shift(block, "x", 1), shift(block, "x", -1)
    sq = sq + lax.ppermute(sq, "y", [(i, i ^ 1) for i in range(4)])
    sq = sq + lax.ppermute(sq, "y", [(i, i ^ 2) for i in range(4)])
    sq, swap = lax.optimization_barrier((sq, mine))
    sq = sq + lax.ppermute(sq, "x", [(i, i ^ 1) for i in range(4)])
    other = lax.ppermute(swap, "core", [(0, 1), (1, 0)])
    got = [block, below, above, shift(below[:HB], "x", 1), shift(above[HB:], "x", -1)]
    sq = sq + lax.ppermute(sq, "x", [(i, i ^ 2) for i in range(4)])
    rel = [x, x + 3, x + 1, x + 2, y, y + 3, y + 1, y + 2]
    order = jnp.concatenate([jnp.stack(rel) % 4, core.reshape(1)]).astype(jnp.int32)
    half = jax.ShapeDtypeStruct((HB, S), jnp.bfloat16)
    h, far0, far1 = stage(
        far_kernel,
        order,
        (*got, sq, gain, mine, other),
        [whole(B, S)] * 3 + [whole(HB, S), whole(B - HB, S), whole(1, N), whole(Q, 128)] + picked(7),
        [jax.ShapeDtypeStruct((Q, N), jnp.bfloat16), half, half],
        [pltpu.VMEM((8, N), jnp.float32)],
        1,
        "far",
    )
    r0, r1 = shift(far0, "y", 1), shift(far1, "y", -1)
    one = jax.ShapeDtypeStruct((M * T, S), jnp.float32)
    plus, minus = stage(
        near_kernel,
        order,
        (h, mine, other, mine, other),
        [whole(Q, N)] + picked(6) + picked(5),
        [one, one],
        [],
        2,
        "near",
    )
    plus, minus, r0, r1 = lax.optimization_barrier((plus, minus, r0, r1))
    plus = jnp.concatenate([plus[:HB] + r0.astype(jnp.float32), plus[HB:]], 0).astype(jnp.bfloat16)
    minus = jnp.concatenate([minus[:HB], minus[HB:] + r1.astype(jnp.float32)], 0).astype(jnp.bfloat16)
    plus, minus, h = lax.optimization_barrier((plus, minus, h))
    (base,) = stage(
        own_kernel,
        order,
        (h, mine, other, block),
        [whole(Q, N)] + picked(4) + [whole(B, S)],
        [one],
        [],
        1,
        "own",
    )
    total = base + shift(plus, "y", 1).astype(jnp.float32) + shift(minus, "y", -1).astype(jnp.float32)
    out = jnp.concatenate([block[: M * T], total.astype(jnp.bfloat16)], 0)
    return out.reshape(2, M, T, S).transpose(0, 1, 3, 2)


def solution(mesh):
    grid = Mesh(mesh.devices.reshape(4, 4, 8, 2), ("x", "y", "z", "core"))
    in_specs = (P(None, ("z", "core"), None), P(None, None, None, ("x", "y")), P())
    out_specs = P(None, None, ("z", "core"), ("x", "y"))
    return jax.shard_map(local, mesh=grid, in_specs=in_specs, out_specs=out_specs, check_vma=False)
```

```python
import functools
import jax
import jax.numpy as jnp
from jax import lax
from jax.experimental import pallas as pl
from jax.experimental.pallas import tpu as pltpu
from jax.sharding import Mesh, PartitionSpec as P

C = 1536
T = 96
R = 480
S = 512
M = 4
B = 400
HB = 192
Q = 384
HR = 240
N = M * S + 128
NT = (((1,), (1,)), ((), ()))


def whole(*shape):
    return pl.BlockSpec(shape, lambda i, *_: (0,) * len(shape))


def gelu(z):
    half = 0.5 * z
    return half + half * jnp.tanh(z * (0.7978845608028654 + 0.035677408136300125 * (z * z)))


def combine(wide):
    n = wide.shape[1]
    total = wide[2 * T : 3 * T]
    for k in (0, 1, 3, 4):
        total = total + pltpu.roll(wide[k * T : (k + 1) * T], (2 - k) % n, 1)
    return total


def first_kernel(info, x_ref, halo_ref, gain_ref, w_ref, o_ref, sq_ref, h_ref, y_ref, hy_ref, hr_ref):
    i = pl.program_id(0)
    start = pl.multiple_of(info[0] * 128, 128)
    off = info[1]
    row = lax.broadcasted_iota(jnp.int32, (T, 256), 0)
    col = lax.broadcasted_iota(jnp.int32, (T, 256), 1)
    pick = jnp.where(col == row + off, 1.0, 0.0).astype(jnp.bfloat16)

    def hidden(v):
        v = v.astype(jnp.float32)
        scale = lax.rsqrt(jnp.sum(v * v, axis=-1, keepdims=True) * (1.0 / C) + 1e-06)
        return gelu(v * scale * gain_ref[...]).astype(jnp.bfloat16)

    @pl.when(i == 0)
    def _():
        hh = hidden(halo_ref[...])
        hy_ref[...] = jnp.zeros_like(hy_ref)
        hr_ref[...] = jnp.zeros_like(hr_ref)
        sq_ref[...] = jnp.zeros_like(sq_ref)
        hy = lax.dot_general(w_ref[...], hh, NT, preferred_element_type=jnp.float32)
        hx = lax.dot_general(pick, halo_ref[:, pl.ds(start, 256)], NT, preferred_element_type=jnp.float32)
        hy_ref[:, 0:32] = hy
        hy_ref[2 * T : 3 * T, 0:32] += hx

    window = pl.ds(start, 256)
    for c in range(2):
        for r in range(c * 256, c * 256 + 256, 16):
            h_ref[r : r + 16, :] = hidden(x_ref[0, r : r + 16, :])
        at = slice(c * 256, c * 256 + 256)
        to = slice(128 + c * 256, 384 + c * 256)
        y_ref[:, to] = lax.dot_general(w_ref[...], h_ref[at, :], NT, preferred_element_type=jnp.float32)
        y_ref[2 * T : 3 * T, to] += lax.dot_general(
            pick, x_ref[0, at, window], NT, preferred_element_type=jnp.float32
        )
    y_ref[:, 0:128] = pltpu.roll(hy_ref[...], lax.rem(252 - 8 * i, 128), 1)
    y_ref[:, 128 + S :] = pltpu.roll(hy_ref[...], lax.rem(252 - 8 * i, 128), 1)
    out = combine(y_ref[...])
    out = out.astype(jnp.bfloat16)
    o_ref[pl.ds(pl.multiple_of(i * T, 16), T), :] = out[:, 128 : 128 + S]
    out = out.astype(jnp.float32)
    squares = jnp.sum(out * out, axis=0, keepdims=True)
    sq_ref[:, pl.ds(pl.multiple_of(i * S, 128), S)] = squares[:, 128 : 128 + S]
    pad = jnp.zeros((32, 128), jnp.float32)
    left = jnp.concatenate([out[:, 0:128], pad], 0).T
    right = jnp.concatenate([out[:, 128 + S :], pad], 0).T
    keep_left = (info[2] > 0).astype(jnp.float32)
    keep_right = (info[3] > 0).astype(jnp.float32)
    lane = lax.broadcasted_iota(jnp.int32, (1, 128), 1) - 4 * i
    turn = lax.rem(4 * i + 2, 128)
    edge = jnp.where((lane == 0) | (lane == 1), pltpu.roll(squares[:, 0:128], turn, 1) * keep_left, 0.0)
    edge += jnp.where((lane == 2) | (lane == 3), pltpu.roll(squares[:, 128 + S :], turn, 1) * keep_right, 0.0)
    sq_ref[:, M * S :] += edge
    line = jnp.concatenate(
        [left[126:127] * keep_left, left[127:128] * keep_left, right[0:1] * keep_right, right[1:2] * keep_right], 1
    )
    hr_ref[pl.ds(i, 1), :] = line
    o_ref[M * T :, :] = hr_ref[...].astype(jnp.bfloat16)


def first(x, halo, gain, w, info):
    return pl.pallas_call(
        first_kernel,
        grid_spec=pltpu.PrefetchScalarGridSpec(
            num_scalar_prefetch=1,
            grid=(M,),
            in_specs=[
                pl.BlockSpec((1, S, C), lambda i, info: (i, 0, 0)),
                whole(32, C),
                whole(1, C),
                pl.BlockSpec((None, R, C), lambda i, info: (0, 0, 0)),
            ],
            out_specs=[whole(B, S), whole(1, N)],
            scratch_shapes=[
                pltpu.VMEM((S, C), jnp.bfloat16),
                pltpu.VMEM((R, S + 256), jnp.float32),
                pltpu.VMEM((R, 128), jnp.float32),
                pltpu.VMEM((16, S), jnp.float32),
            ],
        ),
        out_shape=[jax.ShapeDtypeStruct((B, S), jnp.bfloat16), jax.ShapeDtypeStruct((1, N), jnp.float32)],
        compiler_params=pltpu.CompilerParams(dimension_semantics=("arbitrary",), vmem_limit_bytes=32 << 20),
        cost_estimate=pl.CostEstimate(flops=2 * M * S * R * C, bytes_accessed=2 * M * S * C, transcendentals=M * S * C),
        name="first",
    )(info, x, halo, gain, w)


def prep_kernel(core, w_ref, o_ref):
    for r in range(0, HR, 80):
        v = w_ref[r : r + 80, :].astype(jnp.float32)
        for b in range(4):
            cols = [v[:, (a * 4 + b) * T : (a * 4 + b) * T + T] for a in range(4)]
            o_ref[b, r : r + 80, :] = jnp.concatenate(cols, 1).astype(jnp.bfloat16)


def prep(core, w):
    return pl.pallas_call(
        prep_kernel,
        grid_spec=pltpu.PrefetchScalarGridSpec(
            num_scalar_prefetch=1,
            grid=(1,),
            in_specs=[pl.BlockSpec((None, HR, C), lambda i, core: (1, core[0], 0))],
            out_specs=whole(4, HR, Q),
        ),
        out_shape=jax.ShapeDtypeStruct((4, HR, Q), jnp.bfloat16),
        compiler_params=pltpu.CompilerParams(vmem_limit_bytes=16 << 20),
        cost_estimate=pl.CostEstimate(flops=0, bytes_accessed=4 * HR * C, transcendentals=0),
        name="prep",
    )(core, w)


def join(core, pairs, v_ref):
    for k, (mine_ref, other_ref) in enumerate(pairs):
        v_ref[pl.ds(pl.multiple_of(k * R + core * HR, 16), HR), :] = mine_ref[...]
        v_ref[pl.ds(pl.multiple_of(k * R + HR - core * HR, 16), HR), :] = other_ref[...]


def taps(y_ref, k, j):
    rows = slice(k * R, k * R + R)
    edge = pltpu.roll(y_ref[rows, M * S :], 126 - 4 * j, 1)
    wide = jnp.concatenate([edge, y_ref[rows, j * S : j * S + S], edge], 1)
    return combine(wide)[:, 128 : 128 + S]


def far_kernel(order, a0, a1, a2, a3, a4, sq_ref, gain_ref, wa_ref, wb_ref, h_ref, far0_ref, far1_ref, y_ref, v_ref, s_ref):
    join(order[8], [(wa_ref, wb_ref)], v_ref)
    s_ref[...] = jnp.broadcast_to(lax.rsqrt(sq_ref[...] * (1.0 / C) + 1e-06), s_ref.shape)

    def put(piece, parts, lines):
        dest = pl.multiple_of(order[piece] * T, 16)
        gain = gain_ref[pl.ds(dest, T), :]
        lines = lines.astype(jnp.float32)
        tile = jnp.concatenate(
            [lines[j : j + 1, 128 * q : 128 * q + 128] for j in range(M) for q in range(4)]
            + [jnp.zeros((112, 128), jnp.float32)],
            0,
        )
        h_ref[pl.ds(dest, T), M * S :] = gelu(tile.T[0:T] * s_ref[0:1, M * S :] * gain).astype(jnp.bfloat16)
        for j in range(M):
            ref, row = parts[j]
            for q in range(4):
                lane = slice(j * S + 128 * q, j * S + 128 * q + 128)
                v = ref[row : row + T, 128 * q : 128 * q + 128].astype(jnp.float32)
                h_ref[pl.ds(dest, T), lane] = gelu(v * s_ref[0:1, lane] * gain).astype(jnp.bfloat16)

    for piece, ref in enumerate((a0, a1, a2)):
        put(piece, [(ref, j * T) for j in range(M)], ref[M * T :, :])
    put(3, [(a3, 0), (a3, T), (a4, 0), (a4, T)], a4[HB:, :])
    y_ref[...] = jnp.dot(v_ref[...], h_ref[...], preferred_element_type=jnp.float32)
    for j in range(2):
        far0_ref[j * T : j * T + T, :] = taps(y_ref, 0, j).astype(jnp.bfloat16)
        far1_ref[j * T : j * T + T, :] = taps(y_ref, 0, j + 2).astype(jnp.bfloat16)


def picked(k):
    return [pl.BlockSpec((None, HR, Q), lambda i, order: (order[k], 0, 0))] * 2


def stage(kernel, order, args, in_specs, outs, scratch, count, name):
    return pl.pallas_call(
        kernel,
        grid_spec=pltpu.PrefetchScalarGridSpec(
            num_scalar_prefetch=1,
            grid=(1,),
            in_specs=in_specs,
            out_specs=[whole(*o.shape) for o in outs],
            scratch_shapes=[pltpu.VMEM((count * R, N), jnp.float32), pltpu.VMEM((count * R, Q), jnp.bfloat16)] + scratch,
        ),
        out_shape=outs,
        compiler_params=pltpu.CompilerParams(vmem_limit_bytes=40 << 20),
        cost_estimate=pl.CostEstimate(flops=2 * count * R * Q * N, bytes_accessed=4 * Q * N, transcendentals=0),
        name=name,
    )(order, *args)


def near_kernel(order, h_ref, pa_ref, pb_ref, ma_ref, mb_ref, p_ref, m_ref, y_ref, v_ref):
    join(order[8], [(pa_ref, pb_ref), (ma_ref, mb_ref)], v_ref)
    y_ref[...] = jnp.dot(v_ref[...], h_ref[...], preferred_element_type=jnp.float32)
    for j in range(M):
        p_ref[j * T : j * T + T, :] = taps(y_ref, 0, j)
        m_ref[j * T : j * T + T, :] = taps(y_ref, 1, j)


def own_kernel(order, h_ref, wa_ref, wb_ref, a_ref, o_ref, y_ref, v_ref):
    join(order[8], [(wa_ref, wb_ref)], v_ref)
    y_ref[...] = jnp.dot(v_ref[...], h_ref[...], preferred_element_type=jnp.float32)
    for j in range(M):
        at = slice(j * T, j * T + T)
        o_ref[at, :] = taps(y_ref, 0, j) + a_ref[at, :].astype(jnp.float32)


def shift(value, axis, d):
    return lax.ppermute(value, axis, [(i, (i + d) % 4) for i in range(4)])


def local(inputs, weights, gains):
    x, y, core = lax.axis_index("x"), lax.axis_index("y"), lax.axis_index("core")
    sec = x * 4 + y
    seq = lax.axis_index("z") * 2 + core
    w = pltpu.with_memory_space_constraint(weights.transpose(0, 1, 3, 2).reshape(2, R, C), pltpu.HBM)
    held = pltpu.with_memory_space_constraint(inputs, pltpu.HBM)
    up = [(i, i + 1) for i in range(15)]
    down = [(i + 1, i) for i in range(15)]
    before = lax.ppermute(inputs[:, S - 4 :], ("z", "core"), up)
    after = lax.ppermute(inputs[:, :4], ("z", "core"), down)
    halo = jnp.concatenate([before, after], 1).reshape(32, C)
    send = prep(core.reshape(1).astype(jnp.int32), w)
    block = jnp.minimum(sec * T // 128, 10)
    info = jnp.stack([block, sec * T - block * 128, seq, 15 - seq]).astype(jnp.int32)
    info, send = lax.optimization_barrier((info, send))
    mine = lax.all_to_all(send, "y", 0, 0, tiled=True)
    gain = lax.dynamic_index_in_dim(gains[1].reshape(4, 4, T), y, 1, False).reshape(Q, 1)
    gain = jnp.broadcast_to(gain, (Q, 128))
    block, sq = first(held, halo, gains[0:1], w, info)
    block, sq, mine = lax.optimization_barrier((block, sq, mine))
    other = lax.ppermute(mine, "core", [(0, 1), (1, 0)])
    below, above = shift(block, "x", 1), shift(block, "x", -1)
    got = [block, below, above, shift(below[:HB], "x", 1), shift(above[HB:], "x", -1)]
    for axis, bit in (("y", 1), ("y", 2), ("x", 2), ("x", 1)):
        sq = sq + lax.ppermute(sq, axis, [(i, i ^ bit) for i in range(4)])
    rel = [x, x + 3, x + 1, x + 2, y, y + 3, y + 1, y + 2]
    order = jnp.concatenate([jnp.stack(rel) % 4, core.reshape(1)]).astype(jnp.int32)
    half = jax.ShapeDtypeStruct((HB, S), jnp.bfloat16)
    h, far0, far1 = stage(
        far_kernel,
        order,
        (*got, sq, gain, mine, other),
        [whole(B, S)] * 3 + [whole(HB, S), whole(B - HB, S), whole(1, N), whole(Q, 128)] + picked(7),
        [jax.ShapeDtypeStruct((Q, N), jnp.bfloat16), half, half],
        [pltpu.VMEM((8, N), jnp.float32)],
        1,
        "far",
    )
    r0, r1 = shift(far0, "y", 1), shift(far1, "y", -1)
    one = jax.ShapeDtypeStruct((M * T, S), jnp.float32)
    plus, minus = stage(
        near_kernel,
        order,
        (h, mine, other, mine, other),
        [whole(Q, N)] + picked(6) + picked(5),
        [one, one],
        [],
        2,
        "near",
    )
    plus, minus, r0, r1 = lax.optimization_barrier((plus, minus, r0, r1))
    plus = jnp.concatenate([plus[:HB] + r0.astype(jnp.float32), plus[HB:]], 0).astype(jnp.bfloat16)
    minus = jnp.concatenate([minus[:HB], minus[HB:] + r1.astype(jnp.float32)], 0).astype(jnp.bfloat16)
    plus, minus, h = lax.optimization_barrier((plus, minus, h))
    (base,) = stage(
        own_kernel,
        order,
        (h, mine, other, block),
        [whole(Q, N)] + picked(4) + [whole(B, S)],
        [one],
        [],
        1,
        "own",
    )
    total = base + shift(plus, "y", 1).astype(jnp.float32) + shift(minus, "y", -1).astype(jnp.float32)
    out = jnp.concatenate([block[: M * T], total.astype(jnp.bfloat16)], 0)
    return out.reshape(2, M, T, S).transpose(0, 1, 3, 2)


def solution(mesh):
    grid = Mesh(mesh.devices.reshape(4, 4, 8, 2), ("x", "y", "z", "core"))
    in_specs = (P(None, ("z", "core"), None), P(None, None, None, ("x", "y")), P())
    out_specs = P(None, None, ("z", "core"), ("x", "y"))
    return jax.shard_map(local, mesh=grid, in_specs=in_specs, out_specs=out_specs, check_vma=False)
```
